512 devices in a mesh: elem: 64 (over y, z), sub: 8 (over x, core).
Axes of the slice: x: 4, y: 4, z: 16, core: 2. Of those that a mesh axis runs over, the one named last changes fastest.
Arguments:
- node_ref: float32 [3, 27, 65536], P(None, None, ('elem', 'sub')), may hold values from -0.05 to 24.05, as said below
- cp_pos: float32 [3, 16384], P(None, ('elem', 'sub')), may hold values from 0 to 24
- cp_coef: float32 [3, 16384], P(None, ('elem', 'sub')), may hold values from -0.24 to 0.24
- cp_count: int32 [512], P(('elem', 'sub')), may hold values from 1 to 32, 4096 in all
- u_prev: float32 [5, 27, 65536], P(None, None, ('elem', 'sub')), may hold values from -6 to 6
- right_side: float32 [5, 27, 65536], P(None, None, ('elem', 'sub')), may hold values from -6 to 6
- elem_count: int32 [512], P(('elem', 'sub')), may hold values from 64 to 128, as said below
- face_link: int32 [6, 65536], P(None, ('elem', 'sub')), may hold values from 0 to 1024, as said below
- send_list: int32 [512, 4, 64], P(('elem', 'sub')), may hold values from 0 to 767
- vol_block: float32 [135, 135], replicated, may hold values from -0.3 to 2.3, as said below
- block_inv: float32 [135, 135], replicated, may hold values from -0.1 to 0.44
- lift_matrix: float32 [135, 270], replicated, may hold values from -0.375 to 0.375
Outputs:
- displacement: float32 [3, 27, 65536], P(None, None, ('elem', 'sub'))
- solution: float32 [5, 27, 65536], P(None, None, ('elem', 'sub'))
The draws below stay inside these ranges and needn't reach their ends.
Inputs may be any that keep to these rules, and one draw needn't show every extreme that they name: `node_ref`: coordinates of each element's 3 x 3 x 3 nodes: a lattice of spacing one half shifted by the element's anchor, each node moved by at most 0.05. `elem_count`: one device holds 128 live elements in every draw. `face_link`: a value below 768 names a local trace column, a value from 768 on a received slot, and 1024 a face on the physical boundary. `vol_block`: the element block: twice the identity plus a dense part.
All inputs are finite; a program needn't handle non-finite values. No bound on the sum of `cp_count` on one device may be relied on, other than what follows from the above.
Results may differ from the reference program's by a relative error of at most 0.0003.
Values sent between devices are 32-bit elements; how exact they have to be, the bound alone decides.
No kernel may reach another device: no remote copies, remote signals or barrier semaphores. Data moves between devices by JAX's collectives and lax.ppermute only.
A program may use at most 64 MiB of HBM per device.

```python
import math
import jax
import jax.numpy as jnp
import numpy as np
from jax import lax

NODES = 27
VARS = 5
ELEM_DEV = 128
SEND_SLOTS = 64
CP_SLOT = 32
CTRL_PTS = 4096
CP_ALL = 16384
ELEMS = 65536
ITERS = 3
N_ELEM = 64
N_SUB = 8
DEVICES = 512


def draw_node_ref(key, part):
    anchor_key, noise_key = jax.random.split(key)
    anchors = jax.random.uniform(anchor_key, (3, 1, ELEMS), jnp.float32, 0.0, 23.0)
    node_ids = jnp.arange(27, dtype=jnp.int32)
    lattice = jnp.stack([node_ids % 3, node_ids // 3 % 3, node_ids // 9]).astype(jnp.float32) * 0.5
    jitter = jax.random.uniform(noise_key, (3, 27, ELEMS), jnp.float32, -0.05, 0.05)
    return anchors + lattice[:, :, None] + jitter


def draw_elem_count(key, part):
    count_key, full_key = jax.random.split(key)
    counts = jax.random.randint(count_key, (DEVICES,), ELEM_DEV // 2, ELEM_DEV + 1)
    chosen = jax.random.randint(full_key, (), 0, DEVICES)
    return counts.at[chosen].set(ELEM_DEV).astype(jnp.int32)


def draw_face_link(key, part):
    slots = 6 * ELEM_DEV
    bound = slots + 4 * SEND_SLOTS
    half = ELEM_DEV // 2

    def one_device(device_key):
        perm_key, base_key, edge_key = jax.random.split(device_key, 3)
        shuffled = jax.random.permutation(perm_key, 6 * half)
        chosen = shuffled[:4 * SEND_SLOTS]
        spots = chosen // half * ELEM_DEV + chosen % half
        base = jax.random.randint(base_key, (slots,), 0, slots)
        edges = jax.random.randint(edge_key, (slots,), 0, 16) == 0
        values = jnp.where(edges, bound, base)
        values = values.at[ELEM_DEV - 1].set(bound)
        values = values.at[spots].set(slots + jnp.arange(4 * SEND_SLOTS, dtype=jnp.int32))
        return values.reshape(6, ELEM_DEV)
    stacked = jax.vmap(one_device)(jax.random.split(key, DEVICES))
    return stacked.transpose(1, 0, 2).reshape(6, ELEMS).astype(jnp.int32)


def block_noise(key):
    noise = jax.random.normal(jax.random.fold_in(key, 11), (135, 135), jnp.float32)
    return jnp.clip(0.6 / math.sqrt(135.0) * noise, -0.3, 0.3)


def draw_vol_block(key, part):
    return 2.0 * jnp.eye(135, dtype=jnp.float32) + block_noise(key)


def draw_block_inv(key, part):
    return (jnp.eye(135, dtype=jnp.float32) - block_noise(key) / 3.0) / 3.0


def with_ends(drawn, stream_key, smallest, top_value):
    spot = [jax.random.randint(jax.random.fold_in(stream_key, axis), (), 0, length) for axis, length in enumerate(drawn.shape)]
    longest = drawn.shape.index(max(drawn.shape))
    next_to = spot[:longest] + [(spot[longest] + 1) % drawn.shape[longest]] + spot[longest + 1:]
    return drawn.at[tuple(spot)].set(smallest).at[tuple(next_to)].set(top_value)


def level_of(own_key, dims, cuts, low, top_value):
    def one(dim, shards_of):
        heights = jax.random.uniform(jax.random.fold_in(jax.random.fold_in(own_key, 6), dim), (shards_of,), jnp.float32, low / len(cuts), top_value / len(cuts))
        return jnp.repeat(jnp.exp(heights), dims[dim] // shards_of).reshape((-1,) + (1,) * (len(dims) - dim - 1))

    loudness = one(*cuts[0])
    for cut in cuts[1:]:
        loudness = loudness * one(*cut)
    return loudness


def length_profile(amount, total, most, skew):
    loads = [(1 << 20) // math.isqrt(rank ** skew) + 1 for rank in range(2, amount + 1)]
    spare, given = total - most - (amount - 1), [1] * (amount - 1)
    while spare > 0:
        movable = [i for i in range(amount - 1) if given[i] < most]
        mass, remaining = sum([loads[i] for i in movable]), spare
        for i in movable:
            more = min(most - given[i], max(1, remaining * loads[i] // mass), spare)
            given[i] = given[i] + more
            spare = spare - more
    return np.array([most] + given)


def uneven(rng, number_of, total, most, lean):
    if number_of == 2:
        one = jax.random.randint(rng, (), max(1, total - most), min(most, total - 1) + 1)
        return jnp.stack([one, total - one])
    tallies = jnp.asarray(length_profile(number_of, total, most, lean), jnp.int32)
    couples = (number_of - 1) // 2
    source_of, sink = tallies[1:1 + 2 * couples:2], tallies[2:2 + 2 * couples:2]
    room = jnp.minimum(source_of - 1, most - sink)
    moved = jax.random.randint(jax.random.fold_in(rng, 1), (couples,), 0, 1 << 20) % (room + 1)
    tallies = tallies.at[1:1 + 2 * couples:2].set(source_of - moved).at[2:2 + 2 * couples:2].set(sink + moved)
    return tallies[jax.random.permutation(jax.random.fold_in(rng, 2), number_of)]


def centred(own_key, extent, spread, most, shards=(), held_as=jnp.bfloat16):
    drawn = spread * jax.random.normal(own_key, extent, jnp.float32)
    if shards:
        drawn = drawn * level_of(own_key, extent, shards, -0.22, 0.18)
    return jnp.clip(drawn, -most, most).astype(held_as)


def setup_inputs(seed: int = 0) -> dict:
    key_list = jax.random.split(jax.random.key(seed), 13)
    return {
        "node_ref": draw_node_ref(jax.random.fold_in(key_list[12], 71), 0),
        "cp_pos": jnp.clip(24.0 * jax.random.uniform(key_list[1], (3, CP_ALL), jnp.float32) ** level_of(key_list[1], (3, CP_ALL), ((1, 512),), -0.2, 0.2), 0.0, 24.0),
        "cp_coef": centred(key_list[2], (3, CP_ALL), 0.04, 0.24, ((1, 512),), jnp.float32),
        "cp_count": uneven(key_list[3], DEVICES, CTRL_PTS, CP_SLOT, 2).astype(jnp.int32),
        "u_prev": centred(key_list[4], (VARS, NODES, ELEMS), 1.0, 6.0, ((2, 512),), jnp.float32),
        "right_side": centred(key_list[5], (VARS, NODES, ELEMS), 1.0, 6.0, ((2, 512),), jnp.float32),
        "elem_count": draw_elem_count(jax.random.fold_in(key_list[12], 71), 0),
        "face_link": draw_face_link(jax.random.fold_in(key_list[12], 71), 0),
        "send_list": with_ends(jax.random.randint(key_list[8], (DEVICES, 4, SEND_SLOTS), 0, 6 * ELEM_DEV), jax.random.fold_in(key_list[8], 1), 0, (6 * ELEM_DEV) - 1).astype(jnp.int32),
        "vol_block": draw_vol_block(jax.random.fold_in(key_list[12], 71), 0),
        "block_inv": draw_block_inv(jax.random.fold_in(key_list[12], 71), 0),
        "lift_matrix": centred(key_list[11], (VARS * NODES, 6 * VARS * 9), 270 ** -0.5, 0.375, (), jnp.float32),
    }


HIGH = lax.Precision.HIGHEST
RADIUS = 1.5

def lagrange_tables():
    slopes = np.array([[-1.5, 2.0, -0.5], [-0.5, 0.0, 0.5], [0.5, -2.0, 1.5]])
    single = np.eye(3)
    derivs = np.stack([np.kron(single, np.kron(single, slopes)), np.kron(single, np.kron(slopes, single)), np.kron(slopes, np.eye(9))])
    blending = np.zeros((27, 8))
    for node_id in range(27):
        digits = (node_id % 3, node_id // 3 % 3, node_id // 9)
        for corner in range(8):
            corner_side = (corner % 2, corner // 2 % 2, corner // 4)
            weight = 1.0
            for axis_id in range(3):
                position = digits[axis_id] - 1.0
                if corner_side[axis_id]:
                    weight = weight * (1.0 + position) / 2.0
                else:
                    weight = weight * (1.0 - position) / 2.0
            blending[node_id, corner] = weight
    corner_ids = np.array([2 * (corner % 2) + 6 * (corner // 2 % 2) + 18 * (corner // 4) for corner in range(8)])
    face_ids = []
    for axis_id in range(3):
        for layer_id in (0, 2):
            face_ids.append([node_id for node_id in range(27) if node_id // 3 ** axis_id % 3 == layer_id])
    return (derivs, blending, corner_ids, np.array(face_ids))

def matmul(left, right):
    return jnp.dot(left, right, precision=HIGH, preferred_element_type=jnp.float32)

def radial_sum(corner_major, centers, weights):

    def one_corner(coords):
        dist_sq = (coords[0][None, :] - centers[0][:, None]) ** 2
        dist_sq = dist_sq + (coords[1][None, :] - centers[1][:, None]) ** 2
        dist_sq = dist_sq + (coords[2][None, :] - centers[2][:, None]) ** 2
        ratio = jnp.sqrt(dist_sq) / RADIUS
        inside = jnp.maximum(1.0 - ratio, 0.0)
        kernel = inside ** 4 * (4.0 * ratio + 1.0)
        return matmul(weights, kernel)
    return lax.map(one_corner, corner_major)

def jacobian_metric(moved_nodes, derivs):
    jacobian = jnp.einsum('jmk,ike->ijme', derivs, moved_nodes, precision=HIGH)
    minor_a = jacobian[1, 1] * jacobian[2, 2] - jacobian[1, 2] * jacobian[2, 1]
    minor_b = jacobian[1, 0] * jacobian[2, 2] - jacobian[1, 2] * jacobian[2, 0]
    minor_c = jacobian[1, 0] * jacobian[2, 1] - jacobian[1, 1] * jacobian[2, 0]
    return 8.0 * (jacobian[0, 0] * minor_a - jacobian[0, 1] * minor_b + jacobian[0, 2] * minor_c)

def reference(node_ref, cp_pos, cp_coef, cp_count, u_prev, right_side, elem_count, face_link, send_list, vol_block, block_inv, lift_matrix):
    derivs, blending, corner_ids, face_ids = lagrange_tables()
    derivs = jnp.asarray(derivs, jnp.float32)
    blending = jnp.asarray(blending, jnp.float32)
    slot_ids = jnp.arange(CP_ALL, dtype=jnp.int32)
    live_slot = slot_ids % CP_SLOT < jnp.repeat(cp_count, CP_SLOT)
    ordering = jnp.argsort(jnp.where(live_slot, 0, 1).astype(jnp.int32), stable=True)[:CTRL_PTS]
    centers = cp_pos[:, ordering]
    weights = jnp.where(live_slot[None, :], cp_coef, 0.0)[:, ordering]
    corner_pos = node_ref[:, corner_ids, :]
    per_device = corner_pos.reshape(3, 8, DEVICES, ELEM_DEV).transpose(2, 1, 0, 3)
    corner_disp = lax.map(lambda device_block: radial_sum(device_block, centers, weights), per_device)
    corner_disp = corner_disp.transpose(2, 1, 0, 3).reshape(3, 8, ELEMS)
    displacement = jnp.einsum('nc,ice->ine', blending, corner_disp, precision=HIGH)
    moved_nodes = node_ref + displacement
    metric = jacobian_metric(moved_nodes, derivs)
    scaling = jnp.tile(metric, (5, 1))
    elem_ids = jnp.arange(ELEMS, dtype=jnp.int32)
    live_elem = elem_ids % ELEM_DEV < jnp.repeat(elem_count, ELEM_DEV)
    iterate = jnp.where(live_elem[None, :], u_prev.reshape(135, ELEMS), 0.0)
    source = right_side.reshape(135, ELEMS)
    face_links = face_link.reshape(6, DEVICES, ELEM_DEV).transpose(1, 0, 2)
    blank_sub = jnp.zeros((N_ELEM, 1, 45, SEND_SLOTS), jnp.float32)
    blank_elem = jnp.zeros((1, N_SUB, 45, SEND_SLOTS), jnp.float32)
    for sweep in range(ITERS):
        traces = iterate.reshape(5, 27, ELEMS)[:, face_ids.T, :]
        traces = traces.reshape(45, 6, DEVICES, ELEM_DEV).transpose(2, 0, 1, 3).reshape(DEVICES, 45, 6 * ELEM_DEV)
        packets = jax.vmap(lambda local_table, index_list: jnp.take(local_table, index_list, axis=1))(traces, send_list)
        by_device = packets.transpose(0, 2, 1, 3).reshape(N_ELEM, N_SUB, 4, 45, SEND_SLOTS)
        below_sub = jnp.concatenate([blank_sub, by_device[:, :-1, 0]], axis=1)
        above_sub = jnp.concatenate([by_device[:, 1:, 1], blank_sub], axis=1)
        below_elem = jnp.concatenate([blank_elem, by_device[:-1, :, 2]], axis=0)
        above_elem = jnp.concatenate([by_device[1:, :, 3], blank_elem], axis=0)
        received = jnp.stack([below_sub, above_sub, below_elem, above_elem], axis=2)
        received = received.reshape(DEVICES, 4, 45, SEND_SLOTS).transpose(0, 2, 1, 3).reshape(DEVICES, 45, 4 * SEND_SLOTS)
        full_table = jnp.concatenate([traces, received], axis=2)
        neighbor = jax.vmap(lambda local_table, index_list: jnp.take(local_table, index_list, axis=1, mode='fill', fill_value=0.0))(full_table, face_links)
        neighbor = neighbor.reshape(DEVICES, 270, ELEM_DEV).transpose(1, 0, 2).reshape(270, ELEMS)
        applied = scaling * iterate + matmul(vol_block, iterate) - matmul(lift_matrix, neighbor)
        iterate = jnp.where(live_elem[None, :], iterate + matmul(block_inv, source - applied), 0.0)
    return (displacement, iterate.reshape(5, 27, ELEMS))
```

```python
import functools

import jax
import jax.numpy as jnp
import numpy as np
from jax import lax
from jax.experimental import pallas as pl
from jax.experimental.pallas import tpu as pltpu
from jax.sharding import PartitionSpec as P

ITERS = 3
BOTH = ("elem", "sub")
RADIUS = 1.5
FAR = 1000.0
LANES = 128
STRIP = 512
RUN = 768
TILES = 16
SLOTS = 8
INTERPRET = False
F32, BF16, I32 = jnp.float32, jnp.bfloat16, jnp.int32
VMEM = pltpu.MemorySpace.VMEM
SMEM = pltpu.MemorySpace.SMEM


def node_tables():
    slopes = np.array([[-1.5, 2.0, -0.5], [-0.5, 0.0, 0.5], [0.5, -2.0, 1.5]])
    one = np.eye(3)
    derivs = np.zeros((96, 32), np.float32)
    for axis, full in enumerate(
        (
            np.kron(one, np.kron(one, slopes)),
            np.kron(one, np.kron(slopes, one)),
            np.kron(slopes, np.eye(9)),
        )
    ):
        derivs[32 * axis : 32 * axis + 27, :27] = full
    blending = np.zeros((32, 8), np.float32)
    for node in range(27):
        place = (node % 3 - 1.0, node // 3 % 3 - 1.0, node // 9 - 1.0)
        for corner in range(8):
            weight = 1.0
            for axis in range(3):
                side = 1.0 if corner >> axis & 1 else -1.0
                weight *= (1.0 + side * place[axis]) / 2.0
            blending[node, corner] = weight
    select = np.zeros((288, 136), np.float32)
    for face in range(6):
        axis, layer = face // 2, 2 * (face % 2)
        nodes = [n for n in range(27) if n // 3**axis % 3 == layer]
        for var in range(5):
            for at, node in enumerate(nodes):
                select[48 * face + 9 * var + at, 27 * var + node] = 1.0
    place = np.zeros((270, 288), np.float32)
    for face in range(6):
        for entry in range(45):
            place[6 * entry + face, 48 * face + entry] = 1.0
    return derivs, blending, select, place


CORNERS = [2 * (c & 1) + 6 * (c >> 1 & 1) + 18 * (c >> 2) for c in range(8)]


def hdot(a, b):
    return jnp.dot(a, b, precision=lax.Precision.HIGHEST, preferred_element_type=F32)


def pieces(x, count):
    out = []
    for _ in range(count):
        piece = x.astype(BF16)
        out.append(piece)
        x = x - piece.astype(F32)
    return out


def split_dot(a, b):
    a1, a2 = pieces(a, 2)
    b1, b2 = pieces(b, 2)
    high = jnp.dot(a1, b1, preferred_element_type=F32)
    return high + (jnp.dot(a1, b2, preferred_element_type=F32) + jnp.dot(a2, b1, preferred_element_type=F32))


def pick_dot(a, b, count=2):
    out = None
    for piece in pieces(b, count):
        part = jnp.dot(a, piece, preferred_element_type=F32)
        out = part if out is None else out + part
    return out


def nt_dot(a, b):
    return lax.dot_general(a, b, (((1,), (1,)), ((), ())), preferred_element_type=F32)


def iota(shape, dim):
    return lax.broadcasted_iota(I32, shape, dim)


def flag(mask, dtype=F32):
    return jnp.where(mask, 1.0, 0.0).astype(dtype)


def call(body, out_shape, in_spaces, scratch=(), held=True, **kw):
    def place(s):
        return pltpu.VMEM(s.shape, s.dtype) if held and not INTERPRET else s

    run = pl.pallas_call(
        body,
        out_shape=jax.tree.map(place, out_shape),
        in_specs=[pl.BlockSpec(memory_space=s) for s in in_spaces],
        out_specs=jax.tree.map(lambda _: pl.BlockSpec(memory_space=VMEM), out_shape),
        scratch_shapes=list(scratch),
        interpret=INTERPRET,
        **kw,
    )

    def placed(*args):
        if INTERPRET:
            return run(*args)
        return run(*[pltpu.with_memory_space_constraint(a, s) for a, s in zip(args, in_spaces, strict=True)])

    return placed


def shape_of(*dims, dtype=F32):
    return jax.ShapeDtypeStruct(dims, dtype)


def payload_body(count_ref, pos_ref, coef_ref, out_ref, row_ref):
    count = count_ref[0]
    live = iota((1, 32), 1) < count
    for axis in range(3):
        lanes = slice(32 * axis, 32 * axis + 32)
        row_ref[0:1, lanes] = jnp.where(live, pos_ref[axis : axis + 1, :], FAR)
        row_ref[1:2, lanes] = jnp.where(live, coef_ref[axis : axis + 1, :], 0.0)
    row_ref[0:1, 96:128] = jnp.zeros((1, 32), F32)
    row_ref[1:2, 96:128] = jnp.full((1, 32), count, I32).astype(F32)
    out_ref[...] = jnp.broadcast_to(row_ref[0:2, :][None], out_ref.shape)


def compact_body(in_ref, out_ref, part_ref):
    owners = in_ref.shape[0]
    copies, _, room = out_ref.shape
    first, second = in_ref[:, 0, :], in_ref[:, 1, :]
    wide = jnp.broadcast_to(second[:, 96:97], (owners, LANES))
    below = flag(iota((owners, owners), 1) < iota((owners, owners), 0), BF16)
    above = flag(iota((owners, owners), 0) < iota((owners, owners), 1), BF16)
    start_col = jnp.dot(below, wide.astype(BF16), preferred_element_type=F32)
    pick = flag(iota((8, LANES), 1) == 96, BF16)
    count_row = nt_dot(pick, second.astype(BF16))
    start_row = jnp.dot(count_row.astype(BF16), above, preferred_element_type=F32)
    total = jnp.max(start_row + count_row).astype(I32)
    low, end = start_row[0:1, :], (start_row + count_row)[0:1, :]
    for at, piece in enumerate(pieces(first, 3)):
        part_ref[:, LANES * at : LANES * at + LANES] = piece
    for at, piece in enumerate(pieces(second, 3)):
        part_ref[:, LANES * (3 + at) : LANES * (4 + at)] = piece
    for at, piece in enumerate(pieces(start_col, 2)):
        part_ref[:, LANES * (6 + at) : LANES * (7 + at)] = piece
    feature, group = iota((8, LANES), 0), iota((8, LANES), 1) // 32
    fold_first = flag((feature < 3) & (feature == group), BF16)
    fold_second = flag((feature > 3) & (feature < 7) & (feature == group + 4), BF16)
    strip = min(STRIP, room)
    slot = (iota((strip, LANES), 1) % 32).astype(F32)

    def one_strip(at, carry):
        place = (iota((strip, owners), 0) + at * strip).astype(F32)
        owner = flag((place >= low) & (place < end), BF16)
        found = jnp.dot(owner, part_ref[...], preferred_element_type=F32)
        start = found[:, 6 * LANES : 7 * LANES] + found[:, 7 * LANES :]
        here = (iota((strip, LANES), 0) + at * strip).astype(F32)
        mine = slot == here - start
        out = None
        for k in range(3):
            a = jnp.where(mine, found[:, LANES * k : LANES * k + LANES], 0.0).astype(BF16)
            b = jnp.where(mine, found[:, LANES * (3 + k) : LANES * (4 + k)], 0.0).astype(BF16)
            both = nt_dot(fold_first, a) + nt_dot(fold_second, b)
            out = both if out is None else out + both
        dead = iota((8, strip), 1) + at * strip >= total
        row = iota((8, strip), 0)
        out = jnp.where(dead, jnp.where(row < 3, FAR, 0.0), out)
        square = jnp.sum(jnp.where(row < 3, out * out, 0.0), axis=0, keepdims=True)
        out = jnp.where(row == 3, square, out)
        out = jnp.where(row == 7, total.astype(F32), out)
        out_ref[:, :, pl.ds(pl.multiple_of(at * strip, LANES), strip)] = jnp.broadcast_to(
            out[None], (copies, 8, strip)
        )
        return carry

    lax.fori_loop(0, (total + (strip - 1)) // strip, one_strip, 0)


def radial_displacement(z_ref, node_ref, corner_ref, hit_ref, rank_ref, list_ref, sum_ref, over_ref, over_smem, sem):
    groups, _, room = z_ref.shape
    run = min(RUN, room)
    blocks = run // LANES
    at = [[node_ref[i, k : k + 1, :] for k in CORNERS] for i in range(3)]
    middle, reach = [], [None] * 8
    for i in range(3):
        low = functools.reduce(jnp.minimum, at[i])
        high = functools.reduce(jnp.maximum, at[i])
        middle.append(0.5 * (low + high))
        for c in range(8):
            gap = (at[i][c] - middle[i]) ** 2
            reach[c] = gap if i == 0 else reach[c] + gap
    limit = RADIUS + jnp.sqrt(functools.reduce(jnp.maximum, reach))
    offset = middle[0] ** 2 + middle[1] ** 2 + middle[2] ** 2 - limit * limit - 0.02
    row = iota((LANES, LANES), 0)
    table = jnp.where(row == 3, 1.0, 0.0)
    for i in range(3):
        table = jnp.where(row == i, -2.0 * middle[i], table)
    probe = jnp.transpose(table)[:, 0:8]
    offset = jnp.transpose(jnp.broadcast_to(offset, (LANES, LANES)))
    offset = jnp.concatenate([offset] * blocks, axis=1)
    pick = iota((8, LANES), 0) * TILES + iota((8, LANES), 1) % TILES
    for i in range(3):
        for c in range(8):
            corner_ref[i, 8 * c : 8 * c + 8, :] = jnp.take_along_axis(
                jnp.broadcast_to(at[i][c], (8, LANES)), pick, axis=1
            )
        sum_ref[i] = jnp.zeros((64, LANES), F32)
    counts = [jnp.max(z_ref[g, 7:8, 0:LANES]).astype(I32) for g in range(groups)]
    most = functools.reduce(jnp.maximum, counts)
    source, target = iota((LANES, 2 * LANES), 0), iota((LANES, 2 * LANES), 1)
    same_half = source // 64 == target // 64
    prefix = flag(
        (target < LANES) & same_half & (source <= target)
        | (target >= LANES) & (source // 64 == target - LANES),
        BF16,
    )
    half = iota((TILES, LANES), 1) // 64

    def extract(g, start, block, shift):
        points = z_ref[g, :, pl.ds(pl.multiple_of(start + block * LANES, LANES), LANES)]
        three = jnp.concatenate([p.astype(F32) for p in pieces(points, 3)], axis=0).astype(BF16)
        rank = rank_ref[pl.ds(pl.multiple_of((g * blocks + block) * TILES, TILES), TILES), :]
        entries = []
        for h in range(2):
            key = jnp.where(half == h, rank - shift, 0.0)
            chosen = jnp.concatenate([flag(key == s + 1.0) for s in range(SLOTS)], axis=0).astype(BF16)
            found = nt_dot(three, chosen)
            entries.append(found[0:8] + found[8:16] + found[16:24])
        return entries

    def one_part(part, carry):
        first = part * run
        start = jnp.minimum(first, room - run)
        for g in range(groups):
            points = z_ref[g, :, pl.ds(pl.multiple_of(start, LANES), run)]
            gap = hdot(probe, points) + offset
            best = gap[0:TILES]
            for e in range(1, 8):
                best = jnp.minimum(best, gap[TILES * e : TILES * e + TILES])
            lane = iota((TILES, run), 1) + start
            hit = flag((best <= 0.0) & (lane >= first) & (lane < counts[g]))
            for b in range(blocks):
                hit_ref[(g * blocks + b) * TILES : (g * blocks + b + 1) * TILES, :] = hit[:, LANES * b : LANES * b + LANES]
        hits = hit_ref[...]
        ranks = jnp.dot(hits.astype(BF16), prefix, preferred_element_type=F32)
        rank_ref[...] = jnp.where(hits > 0.0, ranks[:, 0:LANES], -1000.0)
        filled = ranks[:, LANES:].reshape(groups * blocks, TILES, LANES)
        filled = jnp.max(filled, axis=1).astype(I32)
        over_ref[...] = filled
        copy = pltpu.make_async_copy(over_ref, over_smem, sem)
        copy.start()
        length = jnp.int32(0)
        for g in range(groups):
            inside = jnp.clip(counts[g] - start, 0, run)
            for b in range(blocks):
                one, two = extract(g, start, b, 0.0)
                list_ref[length] = one
                length = length + jnp.where(inside > LANES * b, 1, 0)
                list_ref[length] = two
                length = length + jnp.where(inside > LANES * b + 64, 1, 0)
        copy.wait()
        crowded = jnp.max(filled) > SLOTS

        def more(length):
            def block_more(index, length):
                g, b = index // blocks, index % blocks

                def round_more(r, length):
                    one, two = extract(g, start, b, (r * SLOTS).astype(F32))
                    list_ref[length] = one
                    length = length + jnp.where(over_smem[index, 0] > r * SLOTS, 1, 0)
                    list_ref[length] = two
                    length = length + jnp.where(over_smem[index, 1] > r * SLOTS, 1, 0)
                    return length

                rounds = (jnp.maximum(over_smem[index, 0], over_smem[index, 1]) + SLOTS - 1) // SLOTS
                return lax.fori_loop(1, rounds, round_more, length)

            return lax.fori_loop(0, groups * blocks, block_more, length)

        length = lax.cond(crowded, more, lambda n: n, length)
        for e in range(4):
            list_ref[length + e] = jnp.zeros((8, LANES), F32)

        def four(step, carry):
            for i in range(2):
                for c in range(0, 64, 8):
                    total = [sum_ref[axis, c : c + 8, :] for axis in range(3)]
                    place = [corner_ref[axis, c : c + 8, :] for axis in range(3)]
                    for e in range(2):
                        entry = list_ref.at[4 * step + 2 * i + e]
                        gap = [place[axis] - entry[axis : axis + 1, :] for axis in range(3)]
                        square = gap[0] * gap[0] + gap[1] * gap[1] + gap[2] * gap[2]
                        ratio = square * lax.rsqrt(jnp.maximum(square, 1e-20)) * (1.0 / RADIUS)
                        inside = jnp.maximum(1.0 - ratio, 0.0)
                        inside = inside * inside
                        kernel = inside * inside * (4.0 * ratio + 1.0)
                        for axis in range(3):
                            total[axis] = total[axis] + entry[4 + axis : 5 + axis, :] * kernel
                    for axis in range(3):
                        sum_ref[axis, c : c + 8, :] = total[axis]
            return carry

        lax.fori_loop(0, (length + 3) // 4, four, 0)
        return carry

    lax.fori_loop(0, (most + (run - 1)) // run, one_part, 0)
    spread = flag(iota((LANES, LANES), 0) % TILES == iota((LANES, LANES), 1) % TILES, BF16)
    own = iota((8, LANES), 0) == iota((8, LANES), 1) // TILES
    out = []
    for i in range(3):
        total = None
        for piece in pieces(sum_ref[i], 3):
            part = jnp.dot(piece, spread, preferred_element_type=F32)
            total = part if total is None else total + part
        rows = [
            jnp.sum(jnp.where(own, total[8 * c : 8 * c + 8], 0.0), axis=0, keepdims=True) for c in range(8)
        ]
        out.append(jnp.concatenate(rows, axis=0))
    return out


def radial_body(
    z_ref, node_ref, derivs_ref, blend_ref, base_ref, start_ref, minus_inv_ref, count_ref, select_ref, send_ref,
    m_ref, where_ref, q0, q1, q2, q3,
    disp_ref, metric_ref, state_ref, trace_ref, packet_ref,
    corner_ref, hit_ref, rank_ref, list_ref, sum_ref, over_ref, over_smem, sem, nodes_ref, remote_ref,
):
    base = base_ref[...] + from_neighbours(q0, q1, q2, q3, where_ref, m_ref, remote_ref)
    corner = radial_displacement(
        z_ref, node_ref, corner_ref, hit_ref, rank_ref, list_ref, sum_ref, over_ref, over_smem, sem
    )
    nodes_ref[...] = jnp.zeros_like(nodes_ref)
    for i in range(3):
        shift = hdot(blend_ref[...], corner[i])
        disp_ref[i] = shift[0:27]
        nodes_ref[0:27, LANES * i : LANES * i + LANES] = node_ref[i] + shift[0:27]
    jac = hdot(derivs_ref[...], nodes_ref[...])
    j = [[jac[32 * l : 32 * l + 32, LANES * i : LANES * i + LANES] for l in range(3)] for i in range(3)]
    minor_a = j[1][1] * j[2][2] - j[1][2] * j[2][1]
    minor_b = j[1][0] * j[2][2] - j[1][2] * j[2][0]
    minor_c = j[1][0] * j[2][1] - j[1][1] * j[2][0]
    metric = 8.0 * (j[0][0] * minor_a - j[0][1] * minor_b + j[0][2] * minor_c)
    metric_ref[...] = jnp.zeros_like(metric_ref)
    for v in range(5):
        metric_ref[27 * v : 27 * v + 27, :] = metric[0:27]
    state = base + split_dot(minus_inv_ref[...], metric_ref[...] * start_ref[...])
    finish(state, count_ref, select_ref, send_ref, state_ref, trace_ref, packet_ref)


def finish(state, count_ref, select_ref, send_ref, state_ref, trace_ref, packet_ref):
    state = jnp.where(iota(state.shape, 1) < count_ref[0], state, 0.0)
    state_ref[...] = state
    traces = pick_dot(select_ref[...], state, 3)
    for f in range(6):
        trace_ref[f] = traces[48 * f : 48 * f + 48]
    tiles = [traces[48 * f : 48 * f + 48] for f in range(6)]
    for pair in range(2):
        packet_ref[pair] = gather_columns(tiles, send_ref[pair : pair + 1, :], 0)


def gather_columns(tiles, index, first):
    rows = tiles[0].shape[0]
    tile = jnp.broadcast_to(index // LANES - first, (rows, LANES))
    lane = jnp.broadcast_to(index % LANES, (rows, LANES))
    out = jnp.zeros((rows, LANES), F32)
    for t, values in enumerate(tiles):
        out = jnp.where(tile == t, jnp.take_along_axis(values, lane, axis=1), out)
    return out


def from_neighbours(q0, q1, q2, q3, where_ref, m_ref, remote_ref):
    for at, q in enumerate((q0, q1, q2, q3)):
        remote_ref[at // 2, :, 64 * (at % 2) : 64 * (at % 2) + 64] = q[...]
    tiles = [remote_ref[0], remote_ref[1]]
    total = None
    for f in range(6):
        found = gather_columns(tiles, where_ref[f : f + 1, :], 6)
        part = split_dot(m_ref[f], found)
        total = part if total is None else total + part
    return total


def setup_state_body(u_ref, count_ref, select_ref, send_ref, state_ref, trace_ref, packet_ref, flat_ref):
    flat_ref[...] = jnp.zeros_like(flat_ref)
    for v in range(5):
        flat_ref[27 * v : 27 * v + 27, :] = u_ref[v]
    finish(flat_ref[...], count_ref, select_ref, send_ref, state_ref, trace_ref, packet_ref)


def setup_matrix_body(
    vol_ref, inv_ref, lift_ref, place_ref, right_ref, state_ref, trace_ref, where_ref,
    minus_ref, both_ref, m_ref, const_ref, base_ref, flat_ref, wide_ref,
):
    wide_ref[...] = jnp.zeros_like(wide_ref)
    wide_ref[0:135, 0:135] = inv_ref[...]
    inverse = wide_ref[:, 0:136]
    minus_ref[...] = -inverse
    both_ref[...] = jnp.zeros_like(both_ref)
    both_ref[0:135, 0:135] = -hdot(inv_ref[...], vol_ref[...])
    m_ref[...] = jnp.zeros_like(m_ref)
    coupling = hdot(inv_ref[...], lift_ref[...])
    moved = None
    for piece in pieces(coupling, 3):
        part = jnp.dot(piece, place_ref[...], preferred_element_type=F32)
        moved = part if moved is None else moved + part
    for f in range(6):
        m_ref[f, 0:135, :] = moved[:, 48 * f : 48 * f + 48]
    flat_ref[...] = jnp.zeros_like(flat_ref)
    for v in range(5):
        flat_ref[27 * v : 27 * v + 27, :] = right_ref[v]
    const = split_dot(inverse, flat_ref[...])
    const_ref[...] = const
    state = state_ref[...]
    base_ref[...] = state + const + split_dot(both_ref[...], state) + local_part(trace_ref, where_ref, m_ref)


def local_part(trace_ref, where_ref, m_ref):
    tiles = [trace_ref[f] for f in range(6)]
    total = None
    for f in range(6):
        found = gather_columns(tiles, where_ref[f : f + 1, :], 0)
        part = split_dot(m_ref[f], found)
        total = part if total is None else total + part
    return total


def local_body(state_ref, trace_ref, metric_ref, const_ref, minus_ref, both_ref, m_ref, where_ref, out_ref):
    state = state_ref[...]
    out = state + const_ref[...] + split_dot(both_ref[...], state)
    out = out + split_dot(minus_ref[...], metric_ref[...] * state)
    out_ref[...] = out + local_part(trace_ref, where_ref, m_ref)


def sweep_body(
    base_ref, count_ref, select_ref, send_ref, m_ref, where_ref, q0, q1, q2, q3,
    state_ref, trace_ref, packet_ref, remote_ref,
):
    state = base_ref[...] + from_neighbours(q0, q1, q2, q3, where_ref, m_ref, remote_ref)
    finish(state, count_ref, select_ref, send_ref, state_ref, trace_ref, packet_ref)


def last_body(base_ref, count_ref, m_ref, where_ref, q0, q1, q2, q3, out_ref, remote_ref, state_ref):
    state = base_ref[...] + from_neighbours(q0, q1, q2, q3, where_ref, m_ref, remote_ref)
    state_ref[...] = jnp.where(iota(state.shape, 1) < count_ref[0], state, 0.0)
    for v in range(5):
        out_ref[v] = state_ref[27 * v : 27 * v + 27, :]


def exchange(packets):
    out = []
    for q, (axis, step) in enumerate((("sub", 1), ("sub", -1), ("elem", 1), ("elem", -1))):
        size = lax.axis_size(axis)
        pairs = [(i, i + step) for i in range(size) if 0 <= i + step < size]
        packet = packets[q // 2, :, 64 * (q % 2) : 64 * (q % 2) + 64]
        out.append(lax.ppermute(packet, axis, pairs))
    return out


def spread(copies, axis):
    return lax.all_to_all(copies, axis, split_axis=0, concat_axis=0, tiled=True)


def per_device(
    node_ref, cp_pos, cp_coef, cp_count, u_prev, right_side, elem_count, face_link, send_list,
    vol_block, block_inv, lift_matrix,
):
    derivs, blending, select, place = node_tables()
    derivs, blending = jnp.asarray(derivs), jnp.asarray(blending)
    select, place = jnp.asarray(select, BF16), jnp.asarray(place, BF16)
    n_elem, n_sub = lax.axis_size("elem"), lax.axis_size("sub")
    room = n_elem * cp_pos.shape[1]
    send = send_list.reshape(2, LANES)
    state_shape = [shape_of(136, LANES), shape_of(6, 48, LANES), shape_of(2, 48, LANES)]

    copies = call(
        payload_body, shape_of(n_elem, 2, LANES), [SMEM, VMEM, VMEM], [pltpu.VMEM((8, LANES), F32)], name="payload"
    )(cp_count, cp_pos, cp_coef)
    mine = spread(copies, "elem")
    state, traces, packets = call(
        setup_state_body, state_shape, [VMEM, SMEM, VMEM, VMEM], [pltpu.VMEM((136, LANES), F32)], name="setup_state"
    )(u_prev, elem_count, select, send)
    received = exchange(packets)
    minus, both, coupling, const, base = call(
        setup_matrix_body,
        [
            shape_of(136, 136), shape_of(136, 136), shape_of(6, 136, 48),
            shape_of(136, LANES), shape_of(136, LANES),
        ],
        [VMEM] * 8,
        [pltpu.VMEM((136, LANES), F32), pltpu.VMEM((136, 256), F32)],
        name="setup_matrix",
    )(vol_block, block_inv, lift_matrix, place, right_side, state, traces, face_link)
    gathered = call(
        compact_body, shape_of(n_sub, 8, room), [VMEM], [pltpu.VMEM((n_elem, 8 * LANES), BF16)], name="compact"
    )(mine)
    points = spread(gathered, "sub")
    blocks = min(RUN, room) // LANES * n_sub
    displacement, metric, state, traces, packets = call(
        radial_body,
        [shape_of(3, 27, LANES), shape_of(136, LANES), *state_shape],
        [VMEM] * 7 + [SMEM] + [VMEM] * 8,
        [
            pltpu.VMEM((3, 64, LANES), F32),
            pltpu.VMEM((blocks * TILES, LANES), F32),
            pltpu.VMEM((blocks * TILES, LANES), F32),
            pltpu.VMEM((blocks * 16 + 8, 8, LANES), F32),
            pltpu.VMEM((3, 64, LANES), F32),
            pltpu.VMEM((blocks, LANES), I32),
            pltpu.SMEM((blocks, LANES), I32),
            pltpu.SemaphoreType.DMA,
            pltpu.VMEM((32, 3 * LANES), F32),
            pltpu.VMEM((2, 48, LANES), F32),
        ],
        name="radial",
    )(
        points, node_ref, derivs, blending, base, state, minus, elem_count, select, send,
        coupling, face_link, *received,
    )
    for sweep in range(1, ITERS):
        received = exchange(packets)
        base = call(local_body, shape_of(136, LANES), [VMEM] * 8, name="local")(
            state, traces, metric, const, minus, both, coupling, face_link
        )
        scratch = [pltpu.VMEM((2, 48, LANES), F32)]
        if sweep < ITERS - 1:
            state, traces, packets = call(
                sweep_body, state_shape, [VMEM, SMEM] + [VMEM] * 8, scratch, name="sweep"
            )(base, elem_count, select, send, coupling, face_link, *received)
        else:
            solution_out = call(
                last_body,
                shape_of(5, 27, LANES),
                [VMEM, SMEM] + [VMEM] * 6,
                scratch + [pltpu.VMEM((136, LANES), F32)],
                held=False,
                name="last",
            )(base, elem_count, coupling, face_link, *received)
    return displacement, solution_out


def solution(mesh):
    in_specs = (
        P(None, None, BOTH), P(None, BOTH), P(None, BOTH), P(BOTH), P(None, None, BOTH), P(None, None, BOTH),
        P(BOTH), P(None, BOTH), P(BOTH, None, None), P(), P(), P(),
    )
    out_specs = (P(None, None, BOTH), P(None, None, BOTH))
    return jax.shard_map(per_device, mesh=mesh, in_specs=in_specs, out_specs=out_specs, check_vma=False)
```

```python
import functools

import jax
import jax.numpy as jnp
import numpy as np
from jax import lax
from jax.experimental import pallas as pl
from jax.experimental.pallas import tpu as pltpu
from jax.sharding import PartitionSpec as P

ITERS = 3
BOTH = ("elem", "sub")
RADIUS = 1.5
FAR = 1000.0
LANES = 128
STRIP = 768
RUN = 768
PACKET = 384
TILES = 16
SLOTS = 8
INTERPRET = False
F32, BF16, I32 = jnp.float32, jnp.bfloat16, jnp.int32
VMEM = pltpu.MemorySpace.VMEM


def node_tables():
    slopes = np.array([[-1.5, 2.0, -0.5], [-0.5, 0.0, 0.5], [0.5, -2.0, 1.5]])
    one = np.eye(3)
    derivs = np.zeros((96, 32), np.float32)
    for axis, full in enumerate(
        (
            np.kron(one, np.kron(one, slopes)),
            np.kron(one, np.kron(slopes, one)),
            np.kron(slopes, np.eye(9)),
        )
    ):
        derivs[32 * axis : 32 * axis + 27, :27] = full
    blending = np.zeros((32, 8), np.float32)
    for node in range(27):
        place = (node % 3 - 1.0, node // 3 % 3 - 1.0, node // 9 - 1.0)
        for corner in range(8):
            weight = 1.0
            for axis in range(3):
                side = 1.0 if corner >> axis & 1 else -1.0
                weight *= (1.0 + side * place[axis]) / 2.0
            blending[node, corner] = weight
    select = np.zeros((288, 136), np.float32)
    for face in range(6):
        axis, layer = face // 2, 2 * (face % 2)
        nodes = [n for n in range(27) if n // 3**axis % 3 == layer]
        for var in range(5):
            for at, node in enumerate(nodes):
                select[48 * face + 9 * var + at, 27 * var + node] = 1.0
    place = np.zeros((270, 288), np.float32)
    for face in range(6):
        for entry in range(45):
            place[6 * entry + face, 48 * face + entry] = 1.0
    return derivs, blending, select, place


CORNERS = [2 * (c & 1) + 6 * (c >> 1 & 1) + 18 * (c >> 2) for c in range(8)]


def pieces(x, count):
    out = []
    for _ in range(count):
        piece = x.astype(BF16)
        out.append(piece)
        x = x - piece.astype(F32)
    return out


def split_dot(a, b):
    a1, a2 = pieces(a, 2)
    b1, b2 = pieces(b, 2)
    high = jnp.dot(a1, b1, preferred_element_type=F32)
    return high + (jnp.dot(a1, b2, preferred_element_type=F32) + jnp.dot(a2, b1, preferred_element_type=F32))


def pick_dot(a, b, count=2):
    out = None
    for piece in pieces(b, count):
        part = jnp.dot(a, piece, preferred_element_type=F32)
        out = part if out is None else out + part
    return out


def nt_dot(a, b):
    return lax.dot_general(a, b, (((1,), (1,)), ((), ())), preferred_element_type=F32)


def iota(shape, dim):
    return lax.broadcasted_iota(I32, shape, dim)


def flag(mask, dtype=F32):
    return jnp.where(mask, 1.0, 0.0).astype(dtype)


def call(body, out_shape, in_spaces, scratch=(), held=True, out_specs=None, **kw):
    held = held if isinstance(held, list) else jax.tree.map(lambda _: held, out_shape)

    def place(s, stays):
        return pltpu.VMEM(s.shape, s.dtype) if stays and not INTERPRET else s

    run = pl.pallas_call(
        body,
        out_shape=jax.tree.map(place, out_shape, held),
        in_specs=[pl.BlockSpec(memory_space=VMEM) for _ in in_spaces],
        out_specs=out_specs or jax.tree.map(lambda _: pl.BlockSpec(memory_space=VMEM), out_shape),
        scratch_shapes=list(scratch),
        interpret=INTERPRET,
        **kw,
    )

    def placed(*args):
        if INTERPRET:
            return run(*args)
        return run(*[a if s is None else pltpu.with_memory_space_constraint(a, s) for a, s in zip(args, in_spaces, strict=True)])

    return placed


def shape_of(*dims, dtype=F32):
    return jax.ShapeDtypeStruct(dims, dtype)


STATE = [shape_of(136, LANES), shape_of(6, 48, LANES), *[shape_of(24, LANES)] * 4]


def payload_body(count_ref, pos_ref, coef_ref, out_ref, row_ref):
    count = jnp.broadcast_to(count_ref[...], (1, LANES))[:, 0:32]
    live = iota((1, 32), 1) < count
    for axis in range(3):
        lanes = slice(32 * axis, 32 * axis + 32)
        row_ref[0:1, lanes] = jnp.where(live, pos_ref[axis : axis + 1, :], FAR)
        row_ref[1:2, lanes] = jnp.where(live, coef_ref[axis : axis + 1, :], 0.0)
    row_ref[0:1, 96:128] = jnp.zeros((1, 32), F32)
    row_ref[1:2, 96:128] = count.astype(F32)
    out_ref[...] = jnp.broadcast_to(row_ref[0:2, :][None], out_ref.shape)


def compact_body(in_ref, p0, p1, out_ref, part_ref):
    owners = in_ref.shape[0]
    copies, _, room = out_ref.shape
    room = room - PACKET
    me = lax.axis_index("sub")
    odd = me % 2 == 1
    ahead, back = jnp.where(odd, p1[...], p0[...]), jnp.where(odd, p0[...], p1[...])
    for peer in range(copies):
        for at in range(3):
            lanes = slice(room + LANES * at, room + LANES * at + LANES)
            rows = slice(8 * at, 8 * at + 8)
            out_ref[peer, :, lanes] = jnp.where(peer > me, ahead[rows], back[rows])
    first, second = in_ref[:, 0, :], in_ref[:, 1, :]
    wide = jnp.broadcast_to(second[:, 96:97], (owners, LANES))
    below = flag(iota((owners, owners), 1) < iota((owners, owners), 0), BF16)
    above = flag(iota((owners, owners), 0) < iota((owners, owners), 1), BF16)
    start_col = jnp.dot(below, wide.astype(BF16), preferred_element_type=F32)
    pick = flag(iota((8, LANES), 1) == 96, BF16)
    count_row = nt_dot(pick, second.astype(BF16))
    start_row = jnp.dot(count_row.astype(BF16), above, preferred_element_type=F32)
    total = jnp.max(start_row + count_row).astype(I32)
    low, end = start_row[0:1, :], (start_row + count_row)[0:1, :]
    for at, piece in enumerate(pieces(first, 3)):
        part_ref[:, LANES * at : LANES * at + LANES] = piece
    for at, piece in enumerate(pieces(second, 2) + pieces(start_col, 2)):
        part_ref[:, LANES * (3 + at) : LANES * (4 + at)] = piece
    feature, group = iota((8, LANES), 0), iota((8, LANES), 1) // 32
    fold_first = flag((feature < 3) & (feature == group), BF16)
    fold_second = flag((feature > 3) & (feature < 7) & (feature == group + 4), BF16)
    strip = min(STRIP, room)
    slot = (iota((strip, LANES), 1) % 32).astype(F32)

    def one_strip(at, carry):
        base = jnp.minimum(at * strip, room - strip)
        place = (iota((strip, owners), 0) + base).astype(F32)
        owner = flag((place >= low) & (place < end), BF16)
        found = jnp.dot(owner, part_ref[...], preferred_element_type=F32)
        start = found[:, 5 * LANES : 6 * LANES] + found[:, 6 * LANES :]
        here = (iota((strip, LANES), 0) + base).astype(F32)
        mine = slot == here - start
        out = None
        for k in range(3):
            a = jnp.where(mine, found[:, LANES * k : LANES * k + LANES], 0.0).astype(BF16)
            both = nt_dot(fold_first, a)
            if k < 2:
                b = jnp.where(mine, found[:, LANES * (3 + k) : LANES * (4 + k)], 0.0).astype(BF16)
                both = both + nt_dot(fold_second, b)
            out = both if out is None else out + both
        dead = iota((8, strip), 1) + base >= total
        row = iota((8, strip), 0)
        out = jnp.where(dead, jnp.where(row < 3, FAR, 0.0), out)
        square = jnp.sum(jnp.where(row < 3, out * out, 0.0), axis=0, keepdims=True)
        out = jnp.where(row == 3, square, out)
        out = jnp.where(row == 7, total.astype(F32), out)
        out_ref[:, :, pl.ds(pl.multiple_of(base, LANES), strip)] = jnp.broadcast_to(
            out[None], (copies, 8, strip)
        )
        return carry

    lax.fori_loop(0, (total + (strip - 1)) // strip, one_strip, 0)


def radial_displacement(z_ref, node_ref, corner_ref, hit_ref, rank_ref, list_ref, sum_ref, over_ref, over_smem, sem):
    groups, _, room = z_ref.shape
    room = room - PACKET
    run = min(RUN, room)
    blocks = run // LANES
    at = [[node_ref[i, k : k + 1, :] for k in CORNERS] for i in range(3)]
    middle, reach = [], [None] * 8
    for i in range(3):
        low = functools.reduce(jnp.minimum, at[i])
        high = functools.reduce(jnp.maximum, at[i])
        middle.append(0.5 * (low + high))
        for c in range(8):
            gap = (at[i][c] - middle[i]) ** 2
            reach[c] = gap if i == 0 else reach[c] + gap
    limit = RADIUS + jnp.sqrt(functools.reduce(jnp.maximum, reach))
    offset = middle[0] ** 2 + middle[1] ** 2 + middle[2] ** 2 - limit * limit * 1.001 - 0.2
    row = iota((LANES, LANES), 0)
    table = jnp.where((row == 3) | (row == 11), 1.0, 0.0)
    for i in range(3):
        high, low = (p.astype(F32) for p in pieces(-2.0 * middle[i], 2))
        table = jnp.where((row == i) | (row == 8 + i), high, jnp.where(row == 16 + i, low, table))
    probe = jnp.transpose(table)[:, 0:24].astype(BF16)
    offset = jnp.transpose(jnp.broadcast_to(offset, (LANES, LANES)))
    offset = jnp.concatenate([offset] * blocks, axis=1)
    pick = iota((8, LANES), 0) * TILES + iota((8, LANES), 1) % TILES
    for i in range(3):
        for c in range(8):
            corner_ref[i, 8 * c : 8 * c + 8, :] = jnp.take_along_axis(
                jnp.broadcast_to(at[i][c], (8, LANES)), pick, axis=1
            )
        sum_ref[i] = jnp.zeros((64, LANES), F32)
    counts = [jnp.max(z_ref[g, 7:8, 0:LANES]).astype(I32) for g in range(groups)]
    most = functools.reduce(jnp.maximum, counts)
    source, target = iota((LANES, 2 * LANES), 0), iota((LANES, 2 * LANES), 1)
    same_half = source // 64 == target // 64
    prefix = flag(
        (target < LANES) & same_half & (source <= target)
        | (target >= LANES) & (source // 64 == target - LANES),
        BF16,
    )
    half = iota((TILES, LANES), 1) // 64

    def extract(g, start, block, shift):
        points = z_ref[g, :, pl.ds(pl.multiple_of(start + block * LANES, LANES), LANES)]
        three = jnp.concatenate([p.astype(F32) for p in pieces(points, 3)], axis=0).astype(BF16)
        rank = rank_ref[pl.ds(pl.multiple_of((g * blocks + block) * TILES, TILES), TILES), :]
        entries = []
        for h in range(2):
            key = jnp.where(half == h, rank - shift, 0.0)
            chosen = jnp.concatenate([flag(key == s + 1.0) for s in range(SLOTS)], axis=0).astype(BF16)
            found = nt_dot(three, chosen)
            entries.append(found[0:8] + found[8:16] + found[16:24])
        return entries

    def one_part(part, carry):
        first = part * run
        start = jnp.minimum(first, room - run)
        for g in range(groups):
            points = z_ref[g, :, pl.ds(pl.multiple_of(start, LANES), run)]
            high, low = pieces(points, 2)
            both = jnp.concatenate([high.astype(F32), low.astype(F32), high.astype(F32)], axis=0)
            gap = jnp.dot(probe, both.astype(BF16), preferred_element_type=F32) + offset
            best = gap[0:TILES]
            for e in range(1, 8):
                best = jnp.minimum(best, gap[TILES * e : TILES * e + TILES])
            lane = iota((TILES, run), 1) + start
            hit = flag((best <= 0.0) & (lane >= first) & (lane < counts[g]))
            for b in range(blocks):
                hit_ref[(g * blocks + b) * TILES : (g * blocks + b + 1) * TILES, :] = hit[:, LANES * b : LANES * b + LANES]
        hits = hit_ref[...]
        ranks = jnp.dot(hits.astype(BF16), prefix, preferred_element_type=F32)
        rank_ref[...] = jnp.where(hits > 0.0, ranks[:, 0:LANES], -1000.0)
        filled = ranks[:, LANES:].reshape(groups * blocks, TILES, LANES)
        filled = jnp.max(filled, axis=1).astype(I32)
        over_ref[...] = filled
        copy = pltpu.make_async_copy(over_ref, over_smem, sem)
        copy.start()
        length = jnp.int32(0)
        for g in range(groups):
            inside = jnp.clip(counts[g] - start, 0, run)
            for b in range(blocks):
                one, two = extract(g, start, b, 0.0)
                list_ref[length] = one
                length = length + jnp.where(inside > LANES * b, 1, 0)
                list_ref[length] = two
                length = length + jnp.where(inside > LANES * b + 64, 1, 0)
        def more(length):
            def block_more(index, length):
                g, b = index // blocks, index % blocks

                def round_more(r, length):
                    one, two = extract(g, start, b, (r * SLOTS).astype(F32))
                    list_ref[length] = one
                    length = length + jnp.where(over_smem[index, 0] > r * SLOTS, 1, 0)
                    list_ref[length] = two
                    length = length + jnp.where(over_smem[index, 1] > r * SLOTS, 1, 0)
                    return length

                rounds = (jnp.maximum(over_smem[index, 0], over_smem[index, 1]) + SLOTS - 1) // SLOTS
                return lax.fori_loop(1, rounds, round_more, length)

            return lax.fori_loop(0, groups * blocks, block_more, length)

        def four(step, carry):
            for i in range(2):
                for c in range(0, 64, 8):
                    total = [sum_ref[axis, c : c + 8, :] for axis in range(3)]
                    place = [corner_ref[axis, c : c + 8, :] for axis in range(3)]
                    for e in range(2):
                        entry = list_ref.at[4 * step + 2 * i + e]
                        gap = [place[axis] - entry[axis : axis + 1, :] for axis in range(3)]
                        square = gap[0] * gap[0] + gap[1] * gap[1] + gap[2] * gap[2]
                        ratio = square * lax.rsqrt(jnp.maximum(square, 1e-20)) * (1.0 / RADIUS)
                        inside = jnp.maximum(1.0 - ratio, 0.0)
                        inside = inside * inside
                        kernel = inside * inside * (4.0 * ratio + 1.0)
                        for axis in range(3):
                            total[axis] = total[axis] + entry[4 + axis : 5 + axis, :] * kernel
                    for axis in range(3):
                        sum_ref[axis, c : c + 8, :] = total[axis]
            return carry

        def evaluate(length):
            for e in range(4):
                list_ref[length + e] = jnp.zeros((8, LANES), F32)
            lax.fori_loop(0, (length + 3) // 4, four, 0)

        evaluate(length)
        copy.wait()

        @pl.when(jnp.max(filled) > SLOTS)
        def crowded():
            evaluate(more(jnp.int32(0)))

        return carry

    lax.fori_loop(0, (most + (run - 1)) // run, one_part, 0)
    spread = flag(iota((LANES, LANES), 0) % TILES == iota((LANES, LANES), 1) % TILES, BF16)
    own = iota((8, LANES), 0) == iota((8, LANES), 1) // TILES
    out = []
    for i in range(3):
        total = None
        for piece in pieces(sum_ref[i], 2):
            part = jnp.dot(piece, spread, preferred_element_type=F32)
            total = part if total is None else total + part
        rows = [
            jnp.sum(jnp.where(own, total[8 * c : 8 * c + 8], 0.0), axis=0, keepdims=True) for c in range(8)
        ]
        out.append(jnp.concatenate(rows, axis=0))
    return out


def radial_body(
    z_ref, node_ref, derivs_ref, blend_ref, base_ref, start_ref, minus_inv_ref, count_ref, select_ref, send_ref,
    m_ref, where_ref, elem_0, elem_1,
    disp_ref, metric_ref, state_ref, trace_ref, p0, p1, p2, p3,
    corner_ref, hit_ref, rank_ref, list_ref, sum_ref, over_ref, over_smem, sem, nodes_ref, shift_ref, out_sem,
):
    packet_refs = (p0, p1, p2, p3)
    me, last = lax.axis_index("sub"), z_ref.shape[0] - 1
    sides = []
    for step in (-1, 1):
        peer, there = jnp.clip(me + step, 0, last), (me + step >= 0) & (me + step <= last)
        rows = [z_ref[peer, :, z_ref.shape[2] - PACKET + LANES * at :][:, 0:LANES] for at in range(3)]
        sides.append(jnp.where(there, jnp.concatenate(rows, axis=0), 0.0))
    base = base_ref[...] + from_neighbours(*sides, *in_line("elem", elem_0[...], elem_1[...]), where_ref, m_ref)
    corner = radial_displacement(
        z_ref, node_ref, corner_ref, hit_ref, rank_ref, list_ref, sum_ref, over_ref, over_smem, sem
    )
    nodes_ref[...] = jnp.zeros_like(nodes_ref)
    for i in range(3):
        shift = pick_dot(blend_ref[...], corner[i], 2)
        shift_ref[i] = shift[0:27]
        nodes_ref[0:27, LANES * i : LANES * i + LANES] = node_ref[i] + shift[0:27]
    out = pltpu.make_async_copy(shift_ref, disp_ref, out_sem)
    out.start()
    jac = pick_dot(derivs_ref[...], nodes_ref[...], 3)
    j = [[jac[32 * l : 32 * l + 32, LANES * i : LANES * i + LANES] for l in range(3)] for i in range(3)]
    minor_a = j[1][1] * j[2][2] - j[1][2] * j[2][1]
    minor_b = j[1][0] * j[2][2] - j[1][2] * j[2][0]
    minor_c = j[1][0] * j[2][1] - j[1][1] * j[2][0]
    metric = 8.0 * (j[0][0] * minor_a - j[0][1] * minor_b + j[0][2] * minor_c)
    metric_ref[...] = jnp.zeros_like(metric_ref)
    for v in range(5):
        metric_ref[27 * v : 27 * v + 27, :] = metric[0:27]
    state = base + split_dot(minus_inv_ref[...], metric_ref[...] * start_ref[...])
    finish(state, count_ref, select_ref, send_ref, state_ref, trace_ref, packet_refs)
    out.wait()


def finish(state, count_ref, select_ref, send_ref, state_ref, trace_ref, packet_refs):
    state = jnp.where(iota(state.shape, 1) < jnp.broadcast_to(count_ref[...], state.shape), state, 0.0)
    state_ref[...] = state
    traces = pick_dot(select_ref[...], state, 3)
    for f in range(6):
        trace_ref[f] = traces[48 * f : 48 * f + 48]
    tiles = [traces[48 * f : 48 * f + 48] for f in range(6)]
    left = iota((24, LANES), 1) < 64
    for pair in range(2):
        both = gather_columns(tiles, send_ref[pair : pair + 1, :], 0)
        top, bottom = both[0:24], both[24:48]
        ahead = jnp.where(left, top, pltpu.roll(bottom, 64, 1))
        back = jnp.where(left, pltpu.roll(top, 64, 1), bottom)
        odd = lax.axis_index(("sub", "elem")[pair]) % 2 == 1
        packet_refs[2 * pair][...] = jnp.where(odd, back, ahead)
        packet_refs[2 * pair + 1][...] = jnp.where(odd, ahead, back)


def gather_columns(tiles, index, first):
    rows = tiles[0].shape[0]
    tile = jnp.broadcast_to(index // LANES - first, (rows, LANES))
    lane = jnp.broadcast_to(index % LANES, (rows, LANES))
    out = jnp.zeros((rows, LANES), F32)
    for t, values in enumerate(tiles):
        out = jnp.where(tile == t, jnp.take_along_axis(values, lane, axis=1), out)
    return out


def in_line(axis, first, second):
    odd = lax.axis_index(axis) % 2 == 1
    return jnp.where(odd, first, second), jnp.where(odd, second, first)


def from_neighbours(before_sub, behind_sub, before_elem, behind_elem, where_ref, m_ref):
    packets = (before_sub, behind_sub, before_elem, behind_elem)
    total = None
    for f in range(6):
        index = where_ref[f : f + 1, :] - 6 * LANES
        packet = jnp.broadcast_to(jnp.where(index >= 0, index // 64, -1), (24, LANES))
        lane = jnp.broadcast_to(index % 64, (24, LANES))
        halves = []
        for half in range(2):
            found = jnp.zeros((24, LANES), F32)
            for q, values in enumerate(packets):
                found = jnp.where(packet == q, jnp.take_along_axis(values, lane + 64 * half, axis=1), found)
            halves.append(found)
        part = split_dot(m_ref[f], jnp.concatenate(halves, axis=0))
        total = part if total is None else total + part
    return total


def arrived(sub_0, sub_1, elem_0, elem_1, where_ref, m_ref):
    sub = in_line("sub", sub_0[...], sub_1[...])
    return from_neighbours(*sub, *in_line("elem", elem_0[...], elem_1[...]), where_ref, m_ref)


def setup_state_body(u_ref, count_ref, select_ref, send_ref, state_ref, trace_ref, p0, p1, p2, p3, flat_ref):
    packet_refs = (p0, p1, p2, p3)
    flat_ref[...] = jnp.zeros_like(flat_ref)
    for v in range(5):
        flat_ref[27 * v : 27 * v + 27, :] = u_ref[v]
    finish(flat_ref[...], count_ref, select_ref, send_ref, state_ref, trace_ref, packet_refs)


def setup_matrix_body(
    vol_ref, inv_ref, lift_ref, place_ref, right_ref, state_ref, trace_ref, where_ref,
    minus_ref, both_ref, m_ref, const_ref, base_ref, flat_ref, wide_ref,
):
    wide_ref[...] = jnp.zeros_like(wide_ref)
    wide_ref[0:135, 0:135] = inv_ref[...]
    inverse = wide_ref[:, 0:136]
    minus_ref[...] = -inverse
    both_ref[...] = jnp.zeros_like(both_ref)
    both_ref[0:135, 0:135] = -split_dot(inv_ref[...], vol_ref[...])
    m_ref[...] = jnp.zeros_like(m_ref)
    coupling = split_dot(inv_ref[...], lift_ref[...])
    moved = None
    for piece in pieces(coupling, 3):
        part = jnp.dot(piece, place_ref[...], preferred_element_type=F32)
        moved = part if moved is None else moved + part
    for f in range(6):
        m_ref[f, 0:135, :] = moved[:, 48 * f : 48 * f + 48]
    flat_ref[...] = jnp.zeros_like(flat_ref)
    for v in range(5):
        flat_ref[27 * v : 27 * v + 27, :] = right_ref[v]
    const = split_dot(inverse, flat_ref[...])
    const_ref[...] = const
    state = state_ref[...]
    base_ref[...] = state + const + split_dot(both_ref[...], state) + local_part(trace_ref, where_ref, m_ref)


def local_part(trace_ref, where_ref, m_ref):
    tiles = [trace_ref[f] for f in range(6)]
    total = None
    for f in range(6):
        found = gather_columns(tiles, where_ref[f : f + 1, :], 0)
        part = split_dot(m_ref[f], found)
        total = part if total is None else total + part
    return total


def local_body(state_ref, trace_ref, metric_ref, const_ref, minus_ref, both_ref, m_ref, where_ref, out_ref):
    state = state_ref[...]
    out = state + const_ref[...] + split_dot(both_ref[...], state)
    out = out + split_dot(minus_ref[...], metric_ref[...] * state)
    out_ref[...] = out + local_part(trace_ref, where_ref, m_ref)


def sweep_body(
    base_ref, count_ref, select_ref, send_ref, m_ref, where_ref, sub_0, sub_1, elem_0, elem_1,
    state_ref, trace_ref, p0, p1, p2, p3,
):
    packet_refs = (p0, p1, p2, p3)
    state = base_ref[...] + arrived(sub_0, sub_1, elem_0, elem_1, where_ref, m_ref)
    finish(state, count_ref, select_ref, send_ref, state_ref, trace_ref, packet_refs)


def last_body(base_ref, count_ref, m_ref, where_ref, sub_0, sub_1, elem_0, elem_1, out_ref, state_ref):
    state = base_ref[...] + arrived(sub_0, sub_1, elem_0, elem_1, where_ref, m_ref)
    state_ref[...] = jnp.where(iota(state.shape, 1) < jnp.broadcast_to(count_ref[...], state.shape), state, 0.0)
    for v in range(5):
        out_ref[v] = state_ref[27 * v : 27 * v + 27, :]


def exchange(packets, axes=("sub", "elem")):
    out = []
    for axis in axes:
        first = 0 if axis == "sub" else 2
        size = lax.axis_size(axis)
        for turn in range(2):
            partner = [(i ^ 1) if turn == 0 else ((i + 1) ^ 1) - 1 for i in range(size)]
            pairs = [(i, j) for i, j in enumerate(partner) if 0 <= j < size]
            out.append(lax.ppermute(packets[first + turn], axis, pairs))
    return out


def spread(copies, axis):
    return lax.all_to_all(copies, axis, split_axis=0, concat_axis=0, tiled=True)


def radial_call(points, node_ref, derivs, blending, base, state, minus, elem_count, select, send, coupling, face_link, received):
    groups, _, room = points.shape
    blocks = min(RUN, room - PACKET) // LANES * groups
    return call(
        radial_body,
        [shape_of(3, 27, LANES), shape_of(136, LANES), *STATE],
        [VMEM] * 7 + [None] + [VMEM] * 6,
        [
            pltpu.VMEM((3, 64, LANES), F32),
            pltpu.VMEM((blocks * TILES, LANES), F32),
            pltpu.VMEM((blocks * TILES, LANES), F32),
            pltpu.VMEM((blocks * 16 + 8, 8, LANES), F32),
            pltpu.VMEM((3, 64, LANES), F32),
            pltpu.VMEM((blocks, LANES), I32),
            pltpu.SMEM((blocks, LANES), I32),
            pltpu.SemaphoreType.DMA,
            pltpu.VMEM((32, 3 * LANES), F32),
            pltpu.VMEM((3, 27, LANES), F32),
            pltpu.SemaphoreType.DMA,
        ],
        held=[False] + [True] * 7,
        out_specs=[pl.BlockSpec(memory_space=pl.ANY)] + [pl.BlockSpec(memory_space=VMEM)] * 7,
        name="radial",
    )(
        points, node_ref, derivs, blending, base, state, minus, elem_count, select, send,
        coupling, face_link, *received,
    )


def per_device(
    node_ref, cp_pos, cp_coef, cp_count, u_prev, right_side, elem_count, face_link, send_list,
    vol_block, block_inv, lift_matrix,
):
    derivs, blending, select, place = node_tables()
    derivs, blending = jnp.asarray(derivs, BF16), jnp.asarray(blending, BF16)
    select, place = jnp.asarray(select, BF16), jnp.asarray(place, BF16)
    n_elem, n_sub = lax.axis_size("elem"), lax.axis_size("sub")
    room = n_elem * cp_pos.shape[1]
    send = send_list.reshape(2, LANES)

    held_count = elem_count.reshape(1, 1)
    copies = call(
        payload_body, shape_of(n_elem, 2, LANES), [None] * 3, [pltpu.VMEM((8, LANES), F32)], name="payload"
    )(cp_count.reshape(1, 1), cp_pos, cp_coef)
    mine = spread(copies, "elem")
    state, traces, *packets = call(
        setup_state_body, STATE, [VMEM, None, VMEM, VMEM], [pltpu.VMEM((136, LANES), F32)], name="setup_state"
    )(u_prev, held_count, select, send)
    gathered = call(
        compact_body,
        shape_of(n_sub, 8, room + PACKET),
        [VMEM] * 3,
        [pltpu.VMEM((n_elem, 7 * LANES), BF16)],
        name="compact",
    )(mine, packets[0], packets[1])
    points = spread(gathered, "sub")
    received = exchange(packets, ("elem",))
    minus, both, coupling, const, base = call(
        setup_matrix_body,
        [
            shape_of(136, 136), shape_of(136, 136), shape_of(6, 136, 48),
            shape_of(136, LANES), shape_of(136, LANES),
        ],
        [VMEM] * 8,
        [pltpu.VMEM((136, LANES), F32), pltpu.VMEM((136, 256), F32)],
        name="setup_matrix",
    )(vol_block, block_inv, lift_matrix, place, right_side, state, traces, face_link)
    displacement, metric, state, traces, *packets = radial_call(
        points, node_ref, derivs, blending, base, state, minus, held_count, select, send,
        coupling, face_link, received,
    )
    for sweep in range(1, ITERS):
        received = exchange(packets)
        base = call(local_body, shape_of(136, LANES), [VMEM] * 8, name="local")(
            state, traces, metric, const, minus, both, coupling, face_link
        )
        if sweep < ITERS - 1:
            state, traces, *packets = call(sweep_body, STATE, [VMEM, None] + [VMEM] * 8, name="sweep")(
                base, held_count, select, send, coupling, face_link, *received
            )
        else:
            solution_out = call(
                last_body,
                shape_of(5, 27, LANES),
                [VMEM, None] + [VMEM] * 6,
                [pltpu.VMEM((136, LANES), F32)],
                held=False,
                name="last",
            )(base, held_count, coupling, face_link, *received)
    return displacement, solution_out


def solution(mesh):
    in_specs = (
        P(None, None, BOTH), P(None, BOTH), P(None, BOTH), P(BOTH), P(None, None, BOTH), P(None, None, BOTH),
        P(BOTH), P(None, BOTH), P(BOTH, None, None), P(), P(), P(),
    )
    out_specs = (P(None, None, BOTH), P(None, None, BOTH))
    return jax.shard_map(per_device, mesh=mesh, in_specs=in_specs, out_specs=out_specs, check_vma=False)
```

```python
import functools

import jax
import jax.numpy as jnp
import numpy as np
from jax import lax
from jax.experimental import pallas as pl
from jax.experimental.pallas import tpu as pltpu
from jax.sharding import PartitionSpec as P

ITERS = 3
BOTH = ("elem", "sub")
RADIUS = 1.5
FAR = 1000.0
LANES = 128
STRIP = 640
RUN = 768
PACKET = 384
TILES = 16
SLOTS = 8
INTERPRET = False
F32, BF16, I32 = jnp.float32, jnp.bfloat16, jnp.int32
VMEM = pltpu.MemorySpace.VMEM
HBM = pltpu.MemorySpace.HBM


def node_tables():
    slopes = np.array([[-1.5, 2.0, -0.5], [-0.5, 0.0, 0.5], [0.5, -2.0, 1.5]])
    one = np.eye(3)
    derivs = np.zeros((96, 32), np.float32)
    for axis, full in enumerate(
        (
            np.kron(one, np.kron(one, slopes)),
            np.kron(one, np.kron(slopes, one)),
            np.kron(slopes, np.eye(9)),
        )
    ):
        derivs[32 * axis : 32 * axis + 27, :27] = full
    blending = np.zeros((32, 8), np.float32)
    for node in range(27):
        place = (node % 3 - 1.0, node // 3 % 3 - 1.0, node // 9 - 1.0)
        for corner in range(8):
            weight = 1.0
            for axis in range(3):
                side = 1.0 if corner >> axis & 1 else -1.0
                weight *= (1.0 + side * place[axis]) / 2.0
            blending[node, corner] = weight
    select = np.zeros((288, 136), np.float32)
    for face in range(6):
        axis, layer = face // 2, 2 * (face % 2)
        nodes = [n for n in range(27) if n // 3**axis % 3 == layer]
        for var in range(5):
            for at, node in enumerate(nodes):
                select[48 * face + 9 * var + at, 27 * var + node] = 1.0
    place = np.zeros((270, 288), np.float32)
    for face in range(6):
        for entry in range(45):
            place[6 * entry + face, 48 * face + entry] = 1.0
    return derivs, blending, select, place


CORNERS = [2 * (c & 1) + 6 * (c >> 1 & 1) + 18 * (c >> 2) for c in range(8)]


def pieces(x, count):
    out = []
    for _ in range(count):
        piece = x.astype(BF16)
        out.append(piece)
        x = x - piece.astype(F32)
    return out


def stored_dot(a_ref, b):
    b1, b2 = pieces(b, 2)
    high = jnp.dot(a_ref[0], b1, preferred_element_type=F32)
    return high + (jnp.dot(a_ref[0], b2, preferred_element_type=F32) + jnp.dot(a_ref[1], b1, preferred_element_type=F32))


def split_dot(a, b):
    a1, a2 = pieces(a, 2)
    b1, b2 = pieces(b, 2)
    high = jnp.dot(a1, b1, preferred_element_type=F32)
    return high + (jnp.dot(a1, b2, preferred_element_type=F32) + jnp.dot(a2, b1, preferred_element_type=F32))


def pick_dot(a, b, count=2):
    out = None
    for piece in pieces(b, count):
        part = jnp.dot(a, piece, preferred_element_type=F32)
        out = part if out is None else out + part
    return out


def nt_dot(a, b):
    return lax.dot_general(a, b, (((1,), (1,)), ((), ())), preferred_element_type=F32)


def iota(shape, dim):
    return lax.broadcasted_iota(I32, shape, dim)


def flag(mask, dtype=F32):
    return jnp.where(mask, 1.0, 0.0).astype(dtype)


def call(body, out_shape, in_spaces, scratch=(), held=True, in_specs=None, out_specs=None, **kw):
    held = held if isinstance(held, list) else jax.tree.map(lambda _: held, out_shape)

    def place(s, stays):
        return pltpu.VMEM(s.shape, s.dtype) if stays and not INTERPRET else s

    run = pl.pallas_call(
        body,
        out_shape=jax.tree.map(place, out_shape, held),
        in_specs=in_specs or [pl.BlockSpec(memory_space=VMEM) for _ in in_spaces],
        out_specs=out_specs or jax.tree.map(lambda _: pl.BlockSpec(memory_space=VMEM), out_shape),
        scratch_shapes=list(scratch),
        interpret=INTERPRET,
        **kw,
    )

    def placed(*args):
        if INTERPRET:
            return run(*args)
        return run(*[a if s is None else pltpu.with_memory_space_constraint(a, s) for a, s in zip(args, in_spaces, strict=True)])

    return placed


def shape_of(*dims, dtype=F32):
    return jax.ShapeDtypeStruct(dims, dtype)


STATE = [shape_of(136, LANES), shape_of(6, 48, LANES), *[shape_of(24, LANES)] * 4]


def payload_body(count_ref, pos_ref, coef_ref, out_ref, row_ref):
    count = jnp.broadcast_to(count_ref[...], (1, LANES))[:, 0:32]
    live = iota((1, 32), 1) < count
    for axis in range(3):
        lanes = slice(32 * axis, 32 * axis + 32)
        row_ref[0:1, lanes] = jnp.where(live, pos_ref[axis : axis + 1, :], FAR)
        row_ref[1:2, lanes] = jnp.where(live, coef_ref[axis : axis + 1, :], 0.0)
    row_ref[0:1, 96:128] = jnp.zeros((1, 32), F32)
    row_ref[1:2, 96:128] = count.astype(F32)
    out_ref[...] = jnp.broadcast_to(row_ref[0:2, :][None], out_ref.shape)


def compact_body(in_ref, p0, p1, order_ref, out_ref, part_ref):
    owners = in_ref.shape[0]
    copies, _, room = out_ref.shape
    room = room - PACKET
    me = lax.axis_index("sub")
    odd = me % 2 == 1
    ahead, back = jnp.where(odd, p1[...], p0[...]), jnp.where(odd, p0[...], p1[...])
    for peer in range(copies):
        for at in range(3):
            lanes = slice(room + LANES * at, room + LANES * at + LANES)
            rows = slice(8 * at, 8 * at + 8)
            out_ref[peer, :, lanes] = jnp.where(peer > me, ahead[rows], back[rows])
    first, second = in_ref[:, 0, :], in_ref[:, 1, :]
    wide = jnp.broadcast_to(second[:, 96:97], (owners, LANES))
    below = flag(iota((owners, owners), 1) < iota((owners, owners), 0), BF16)
    above = flag(iota((owners, owners), 0) < iota((owners, owners), 1), BF16)
    start_col = jnp.dot(below, wide.astype(BF16), preferred_element_type=F32)
    pick = flag(iota((8, LANES), 1) == 96, BF16)
    count_row = nt_dot(pick, second.astype(BF16))
    start_row = jnp.dot(count_row.astype(BF16), above, preferred_element_type=F32)
    low, end = start_row[0:1, :], (start_row + count_row)[0:1, :]
    total = jnp.max(end, axis=1, keepdims=True)
    for at, piece in enumerate(pieces(first, 3)):
        part_ref[:, LANES * at : LANES * at + LANES] = piece
    for at, piece in enumerate(pieces(second, 2) + pieces(start_col, 2)):
        part_ref[:, LANES * (3 + at) : LANES * (4 + at)] = piece
    feature, group = iota((8, LANES), 0), iota((8, LANES), 1) // 32
    fold_first = flag((feature < 3) & (feature == group), BF16)
    fold_second = flag((feature > 3) & (feature < 7) & (feature == group + 4), BF16)
    strip = min(STRIP, room)
    slot = (iota((strip, LANES), 1) % 32).astype(F32)

    def one_strip(at, carry):
        base = min(at * strip, room - strip) if isinstance(at, int) else jnp.minimum(at * strip, room - strip)
        place = (iota((strip, owners), 0) + base).astype(F32)
        owner = flag((place >= low) & (place < end), BF16)
        found = jnp.dot(owner, part_ref[...], preferred_element_type=F32)
        start = found[:, 5 * LANES : 6 * LANES] + found[:, 6 * LANES :]
        here = (iota((strip, LANES), 0) + base).astype(F32)
        mine = slot == here - start
        out = None
        for k in range(3):
            a = jnp.where(mine, found[:, LANES * k : LANES * k + LANES], 0.0).astype(BF16)
            both = nt_dot(fold_first, a)
            if k < 2:
                b = jnp.where(mine, found[:, LANES * (3 + k) : LANES * (4 + k)], 0.0).astype(BF16)
                both = both + nt_dot(fold_second, b)
            out = both if out is None else out + both
        dead = (iota((8, strip), 1) + base).astype(F32) >= total
        row = iota((8, strip), 0)
        out = jnp.where(dead, jnp.where(row < 3, FAR, 0.0), out)
        square = jnp.sum(jnp.where(row < 3, out * out, 0.0), axis=0, keepdims=True)
        out = jnp.where(row == 3, square, out)
        out = jnp.where(row == 7, total, out)
        out_ref[:, :, pl.ds(base if isinstance(base, int) else pl.multiple_of(base, LANES), strip)] = jnp.broadcast_to(
            out[None], (copies, 8, strip)
        )
        return carry

    one_strip(0, 0)
    strips = (jnp.max(total).astype(I32) + (strip - 1)) // strip
    lax.fori_loop(1, strips, one_strip, 0)


def radial_displacement(z_ref, node_ref, corner_ref, hit_ref, rank_ref, list_ref, sum_ref, over_ref, over_smem, sem):
    groups, _, room = z_ref.shape
    room = room - PACKET
    run = min(RUN, room)
    blocks = run // LANES
    at = [[node_ref[i, k : k + 1, :] for k in CORNERS] for i in range(3)]
    middle, reach = [], [None] * 8
    for i in range(3):
        low = functools.reduce(jnp.minimum, at[i])
        high = functools.reduce(jnp.maximum, at[i])
        middle.append(0.5 * (low + high))
        for c in range(8):
            gap = (at[i][c] - middle[i]) ** 2
            reach[c] = gap if i == 0 else reach[c] + gap
    limit = RADIUS + jnp.sqrt(functools.reduce(jnp.maximum, reach))
    offset = middle[0] ** 2 + middle[1] ** 2 + middle[2] ** 2 - limit * limit * 1.001 - 0.2
    row = iota((LANES, LANES), 0)
    table = jnp.where((row == 3) | (row == 11), 1.0, 0.0)
    for i in range(3):
        high, low = (p.astype(F32) for p in pieces(-2.0 * middle[i], 2))
        table = jnp.where((row == i) | (row == 8 + i), high, jnp.where(row == 16 + i, low, table))
    probe = jnp.transpose(table)[:, 0:24].astype(BF16)
    offset = jnp.transpose(jnp.broadcast_to(offset, (LANES, LANES)))
    offset = jnp.concatenate([offset] * blocks, axis=1)
    pick = iota((8, LANES), 0) * TILES + iota((8, LANES), 1) % TILES
    for i in range(3):
        for c in range(8):
            corner_ref[i, 8 * c : 8 * c + 8, :] = jnp.take_along_axis(
                jnp.broadcast_to(at[i][c], (8, LANES)), pick, axis=1
            ) * (1.0 / RADIUS)
        sum_ref[i] = jnp.zeros((64, LANES), F32)
    counts = [jnp.max(z_ref[g, 7:8, 0:LANES]).astype(I32) for g in range(groups)]
    most = functools.reduce(jnp.maximum, counts)
    source, target = iota((LANES, 2 * LANES), 0), iota((LANES, 2 * LANES), 1)
    same_half = source // 64 == target // 64
    prefix = flag(
        (target < LANES) & same_half & (source <= target)
        | (target >= LANES) & (source // 64 == target - LANES),
        BF16,
    )
    half = iota((TILES, LANES), 1) // 64

    def extract(g, start, block, shift):
        points = z_ref[g, :, pl.ds(pl.multiple_of(start + block * LANES, LANES), LANES)]
        three = jnp.concatenate([p.astype(F32) for p in pieces(points, 3)], axis=0).astype(BF16)
        rank = rank_ref[pl.ds(pl.multiple_of((g * blocks + block) * TILES, TILES), TILES), :]
        entries = []
        for h in range(2):
            key = jnp.where(half == h, rank - shift, 0.0)
            chosen = jnp.concatenate([flag(key == s + 1.0) for s in range(SLOTS)], axis=0).astype(BF16)
            found = nt_dot(three, chosen)
            found = found[0:8] + found[8:16] + found[16:24]
            entries.append(jnp.where(iota((8, LANES), 0) < 4, found * (1.0 / RADIUS), found * 4.0))
        return entries

    def one_part(part, carry):
        first = part * run
        start = jnp.minimum(first, room - run)
        for g in range(groups):
            points = z_ref[g, :, pl.ds(pl.multiple_of(start, LANES), run)]
            high, low = pieces(points, 2)
            both = jnp.concatenate([high.astype(F32), low.astype(F32), high.astype(F32)], axis=0)
            gap = jnp.dot(probe, both.astype(BF16), preferred_element_type=F32) + offset
            best = gap[0:TILES]
            for e in range(1, 8):
                best = jnp.minimum(best, gap[TILES * e : TILES * e + TILES])
            lane = iota((TILES, run), 1) + start
            hit = flag((best <= 0.0) & (lane >= first) & (lane < counts[g]))
            for b in range(blocks):
                hit_ref[(g * blocks + b) * TILES : (g * blocks + b + 1) * TILES, :] = hit[:, LANES * b : LANES * b + LANES]
        hits = hit_ref[...]
        ranks = jnp.dot(hits.astype(BF16), prefix, preferred_element_type=F32)
        rank_ref[...] = jnp.where(hits > 0.0, ranks[:, 0:LANES], -1000.0)
        filled = ranks[:, LANES:].reshape(groups * blocks, TILES, LANES)
        filled = jnp.max(filled, axis=1).astype(I32)
        over_ref[...] = filled
        copy = pltpu.make_async_copy(over_ref, over_smem, sem)
        copy.start()
        length = jnp.int32(0)
        for g in range(groups):
            inside = jnp.clip(counts[g] - start, 0, run)
            for b in range(blocks):
                one, two = extract(g, start, b, 0.0)
                list_ref[length] = one
                length = length + jnp.where(inside > LANES * b, 1, 0)
                list_ref[length] = two
                length = length + jnp.where(inside > LANES * b + 64, 1, 0)
        def more(length):
            def block_more(index, length):
                g, b = index // blocks, index % blocks

                def round_more(r, length):
                    one, two = extract(g, start, b, (r * SLOTS).astype(F32))
                    list_ref[length] = one
                    length = length + jnp.where(over_smem[index, 0] > r * SLOTS, 1, 0)
                    list_ref[length] = two
                    length = length + jnp.where(over_smem[index, 1] > r * SLOTS, 1, 0)
                    return length

                rounds = (jnp.maximum(over_smem[index, 0], over_smem[index, 1]) + SLOTS - 1) // SLOTS
                return lax.fori_loop(1, rounds, round_more, length)

            return lax.fori_loop(0, groups * blocks, block_more, length)

        def four(step, carry):
            for i in range(2):
                for c in range(0, 64, 8):
                    total = [sum_ref[axis, c : c + 8, :] for axis in range(3)]
                    place = [corner_ref[axis, c : c + 8, :] for axis in range(3)]
                    for e in range(2):
                        entry = list_ref.at[4 * step + 2 * i + e]
                        gap = [place[axis] - entry[axis : axis + 1, :] for axis in range(3)]
                        square = gap[0] * gap[0] + gap[1] * gap[1] + gap[2] * gap[2]
                        ratio = square * lax.rsqrt(jnp.maximum(square, 1e-20))
                        inside = jnp.maximum(1.0 - ratio, 0.0)
                        inside = inside * inside
                        kernel = inside * inside * (ratio + 0.25)
                        for axis in range(3):
                            total[axis] = total[axis] + entry[4 + axis : 5 + axis, :] * kernel
                    for axis in range(3):
                        sum_ref[axis, c : c + 8, :] = total[axis]
            return carry

        def evaluate(length):
            for e in range(4):
                list_ref[length + e] = jnp.zeros((8, LANES), F32)
            lax.fori_loop(0, (length + 3) // 4, four, 0)

        evaluate(length)
        copy.wait()

        @pl.when(jnp.max(filled) > SLOTS)
        def crowded():
            evaluate(more(jnp.int32(0)))

        return carry

    lax.fori_loop(0, (most + (run - 1)) // run, one_part, 0)
    spread = flag(iota((LANES, LANES), 0) % TILES == iota((LANES, LANES), 1) % TILES, BF16)
    own = iota((8, LANES), 0) == iota((8, LANES), 1) // TILES
    out = []
    for i in range(3):
        total = None
        for piece in pieces(sum_ref[i], 2):
            part = jnp.dot(piece, spread, preferred_element_type=F32)
            total = part if total is None else total + part
        rows = [
            jnp.sum(jnp.where(own, total[8 * c : 8 * c + 8], 0.0), axis=0, keepdims=True) for c in range(8)
        ]
        out.append(jnp.concatenate(rows, axis=0))
    return out


def radial_body(
    z_ref, node_ref, derivs_ref, blend_ref, base_ref, start_ref, minus_inv_ref, count_ref, select_ref, send_ref,
    m_ref, where_ref, elem_0, elem_1,
    disp_ref, metric_ref, state_ref, trace_ref, p0, p1, p2, p3,
    corner_ref, hit_ref, rank_ref, list_ref, sum_ref, over_ref, over_smem, sem, nodes_ref, shift_ref, out_sem,
):
    packet_refs = (p0, p1, p2, p3)
    me, last = lax.axis_index("sub"), z_ref.shape[0] - 1
    sides = []
    for step in (-1, 1):
        peer, there = jnp.clip(me + step, 0, last), (me + step >= 0) & (me + step <= last)
        rows = [z_ref[peer, :, z_ref.shape[2] - PACKET + LANES * at :][:, 0:LANES] for at in range(3)]
        sides.append(jnp.where(there, jnp.concatenate(rows, axis=0), 0.0))
    base = base_ref[...] + from_neighbours(*sides, *in_line("elem", elem_0[...], elem_1[...]), where_ref, m_ref)
    corner = radial_displacement(
        z_ref, node_ref, corner_ref, hit_ref, rank_ref, list_ref, sum_ref, over_ref, over_smem, sem
    )
    nodes_ref[...] = jnp.zeros_like(nodes_ref)
    for i in range(3):
        shift = pick_dot(blend_ref[...], corner[i], 2)
        shift_ref[i] = shift[0:27]
        nodes_ref[0:27, LANES * i : LANES * i + LANES] = node_ref[i] + shift[0:27]
    out = pltpu.make_async_copy(shift_ref, disp_ref, out_sem)
    out.start()
    jac = pick_dot(derivs_ref[...], nodes_ref[...], 3)
    j = [[jac[32 * l : 32 * l + 32, LANES * i : LANES * i + LANES] for l in range(3)] for i in range(3)]
    minor_a = j[1][1] * j[2][2] - j[1][2] * j[2][1]
    minor_b = j[1][0] * j[2][2] - j[1][2] * j[2][0]
    minor_c = j[1][0] * j[2][1] - j[1][1] * j[2][0]
    metric = 8.0 * (j[0][0] * minor_a - j[0][1] * minor_b + j[0][2] * minor_c)
    metric_ref[...] = jnp.zeros_like(metric_ref)
    for v in range(5):
        metric_ref[27 * v : 27 * v + 27, :] = metric[0:27]
    state = base + stored_dot(minus_inv_ref, metric_ref[...] * start_ref[...])
    finish(state, count_ref, select_ref, send_ref, state_ref, trace_ref, packet_refs)
    out.wait()


def finish(state, count_ref, select_ref, send_ref, state_ref, trace_ref, packet_refs):
    state = jnp.where(iota(state.shape, 1) < jnp.broadcast_to(count_ref[...], state.shape), state, 0.0)
    state_ref[...] = state
    traces = pick_dot(select_ref[...], state, 2)
    for f in range(6):
        trace_ref[f] = traces[48 * f : 48 * f + 48]
    tiles = [traces[48 * f : 48 * f + 48] for f in range(6)]
    left = iota((24, LANES), 1) < 64
    for pair in range(2):
        both = gather_columns(tiles, send_ref[pair : pair + 1, :], 0)
        top, bottom = both[0:24], both[24:48]
        ahead = jnp.where(left, top, pltpu.roll(bottom, 64, 1))
        back = jnp.where(left, pltpu.roll(top, 64, 1), bottom)
        odd = lax.axis_index(("sub", "elem")[pair]) % 2 == 1
        packet_refs[2 * pair][...] = jnp.where(odd, back, ahead)
        packet_refs[2 * pair + 1][...] = jnp.where(odd, ahead, back)


def gather_columns(tiles, index, first):
    rows = tiles[0].shape[0]
    tile = jnp.broadcast_to(index // LANES - first, (rows, LANES))
    lane = jnp.broadcast_to(index % LANES, (rows, LANES))
    out = jnp.zeros((rows, LANES), F32)
    for t, values in enumerate(tiles):
        out = jnp.where(tile == t, jnp.take_along_axis(values, lane, axis=1), out)
    return out


def in_line(axis, first, second):
    odd = lax.axis_index(axis) % 2 == 1
    return jnp.where(odd, first, second), jnp.where(odd, second, first)


def from_neighbours(before_sub, behind_sub, before_elem, behind_elem, where_ref, m_ref):
    packets = (before_sub, behind_sub, before_elem, behind_elem)
    columns = []
    for f in range(6):
        index = where_ref[f : f + 1, :] - 6 * LANES
        packet = jnp.broadcast_to(jnp.where(index >= 0, index // 64, -1), (24, LANES))
        lane = jnp.broadcast_to(index % 64, (24, LANES))
        halves = []
        for half in range(2):
            found = jnp.zeros((24, LANES), F32)
            for q, values in enumerate(packets):
                found = jnp.where(packet == q, jnp.take_along_axis(values, lane + 64 * half, axis=1), found)
            halves.append(found)
        columns += halves
    return stored_dot(m_ref, jnp.concatenate(columns, axis=0))


def arrived(sub_0, sub_1, elem_0, elem_1, where_ref, m_ref):
    sub = in_line("sub", sub_0[...], sub_1[...])
    return from_neighbours(*sub, *in_line("elem", elem_0[...], elem_1[...]), where_ref, m_ref)


def setup_body(
    u_ref, count_ref, select_ref, send_ref, vol_ref, inv_ref, lift_ref, place_ref, right_ref, where_ref,
    state_ref, trace_ref, p0, p1, p2, p3, held_ref, sent_ref, link_ref, minus_ref, both_ref, m_ref, const_ref, base_ref,
    flat_ref, wide_ref,
):
    held_ref[...] = jnp.broadcast_to(count_ref[...], held_ref.shape)
    sent_ref[...] = send_ref[...]
    link_ref[...] = where_ref[...]
    flat_ref[...] = jnp.zeros_like(flat_ref)
    for v in range(5):
        flat_ref[27 * v : 27 * v + 27, :] = u_ref[v]
    finish(flat_ref[...], held_ref, select_ref, send_ref, state_ref, trace_ref, (p0, p1, p2, p3))
    wide_ref[...] = jnp.zeros_like(wide_ref)
    wide_ref[0:135, 0:135] = inv_ref[...]
    inverse = wide_ref[:, 0:136]
    wide_ref[0:135, 0:135] = -split_dot(inv_ref[...], vol_ref[...])
    for k, piece in enumerate(pieces(-inverse, 2)):
        minus_ref[k] = piece
    for k, piece in enumerate(pieces(wide_ref[:, 0:136], 2)):
        both_ref[k] = piece
    coupling = split_dot(inverse[:, 0:135], lift_ref[...])
    moved = [jnp.dot(piece, place_ref[...], preferred_element_type=F32) for piece in pieces(coupling, 2)]
    for k in range(2):
        m_ref[k] = moved[k].astype(BF16)
    flat_ref[...] = jnp.zeros_like(flat_ref)
    for v in range(5):
        flat_ref[27 * v : 27 * v + 27, :] = right_ref[v]
    const = split_dot(inverse, flat_ref[...])
    const_ref[...] = const
    state = state_ref[...]
    base_ref[...] = state + const + stored_dot(both_ref, state) + local_part(trace_ref, where_ref, m_ref)


def local_part(trace_ref, where_ref, m_ref):
    tiles = [trace_ref[f] for f in range(6)]
    columns = [gather_columns(tiles, where_ref[f : f + 1, :], 0) for f in range(6)]
    return stored_dot(m_ref, jnp.concatenate(columns, axis=0))


def local_body(state_ref, trace_ref, metric_ref, const_ref, minus_ref, both_ref, m_ref, where_ref, out_ref):
    state = state_ref[...]
    out = state + const_ref[...] + stored_dot(both_ref, state)
    out = out + stored_dot(minus_ref, metric_ref[...] * state)
    out_ref[...] = out + local_part(trace_ref, where_ref, m_ref)


def sweep_body(
    base_ref, count_ref, select_ref, send_ref, m_ref, where_ref, sub_0, sub_1, elem_0, elem_1,
    state_ref, trace_ref, p0, p1, p2, p3,
):
    packet_refs = (p0, p1, p2, p3)
    state = base_ref[...] + arrived(sub_0, sub_1, elem_0, elem_1, where_ref, m_ref)
    finish(state, count_ref, select_ref, send_ref, state_ref, trace_ref, packet_refs)


def last_body(base_ref, count_ref, m_ref, where_ref, sub_0, sub_1, elem_0, elem_1, out_ref, state_ref):
    state = base_ref[...] + arrived(sub_0, sub_1, elem_0, elem_1, where_ref, m_ref)
    state_ref[...] = jnp.where(iota(state.shape, 1) < jnp.broadcast_to(count_ref[...], state.shape), state, 0.0)
    for v in range(5):
        out_ref[v] = state_ref[27 * v : 27 * v + 27, :]


def exchange(packets, axes=("sub", "elem")):
    out = []
    for axis in axes:
        first = 0 if axis == "sub" else 2
        size = lax.axis_size(axis)
        for turn in range(2):
            partner = [(i ^ 1) if turn == 0 else ((i + 1) ^ 1) - 1 for i in range(size)]
            pairs = [(i, j) for i, j in enumerate(partner) if 0 <= j < size]
            out.append(lax.ppermute(packets[first + turn], axis, pairs))
    return out


def spread(copies, axis):
    return lax.all_to_all(copies, axis, split_axis=0, concat_axis=0, tiled=True)


def radial_call(points, node_ref, derivs, blending, base, state, minus, elem_count, select, send, coupling, face_link, received):
    groups, _, room = points.shape
    blocks = min(RUN, room - PACKET) // LANES * groups
    return call(
        radial_body,
        [shape_of(3, 27, LANES), shape_of(136, LANES), *STATE],
        [VMEM] * 14,
        [
            pltpu.VMEM((3, 64, LANES), F32),
            pltpu.VMEM((blocks * TILES, LANES), F32),
            pltpu.VMEM((blocks * TILES, LANES), F32),
            pltpu.VMEM((blocks * 16 + 8, 8, LANES), F32),
            pltpu.VMEM((3, 64, LANES), F32),
            pltpu.VMEM((blocks, LANES), I32),
            pltpu.SMEM((blocks, LANES), I32),
            pltpu.SemaphoreType.DMA,
            pltpu.VMEM((32, 3 * LANES), F32),
            pltpu.VMEM((3, 27, LANES), F32),
            pltpu.SemaphoreType.DMA,
        ],
        held=[False] + [True] * 7,
        out_specs=[pl.BlockSpec(memory_space=pl.ANY)] + [pl.BlockSpec(memory_space=VMEM)] * 7,
        name="radial",
    )(
        points, node_ref, derivs, blending, base, state, minus, elem_count, select, send,
        coupling, face_link, *received,
    )


def per_device(
    node_ref, cp_pos, cp_coef, cp_count, u_prev, right_side, elem_count, face_link, send_list,
    vol_block, block_inv, lift_matrix,
):
    derivs, blending, select, place = node_tables()
    derivs, blending = jnp.asarray(derivs, BF16), jnp.asarray(blending, BF16)
    select, place = jnp.asarray(select, BF16), jnp.asarray(place, BF16)
    n_elem, n_sub = lax.axis_size("elem"), lax.axis_size("sub")
    room = n_elem * cp_pos.shape[1]
    send = send_list.reshape(2, LANES)

    copies = call(
        payload_body, shape_of(n_elem, 2, LANES), [None] * 3, [pltpu.VMEM((8, LANES), F32)], name="payload"
    )(cp_count.reshape(1, 1), cp_pos, cp_coef)
    mine = spread(copies, "elem")
    *first, held_count, sent, link, minus, both, coupling, const, base = call(
        setup_body,
        [
            *STATE, shape_of(1, LANES, dtype=I32), shape_of(2, LANES, dtype=I32), shape_of(6, LANES, dtype=I32),
            shape_of(2, 136, 136, dtype=BF16), shape_of(2, 136, 136, dtype=BF16), shape_of(2, 136, 288, dtype=BF16),
            shape_of(136, LANES), shape_of(136, LANES),
        ],
        [None, None, HBM, None, HBM, HBM, HBM, HBM, HBM, HBM],
        [pltpu.VMEM((136, LANES), F32), pltpu.VMEM((136, 256), F32)],
        name="setup",
    )(
        u_prev, elem_count.reshape(1, 1), select, send, vol_block, block_inv, lift_matrix, place, right_side, face_link
    )
    state, traces, *packets = first
    gathered = call(
        compact_body,
        shape_of(n_sub, 8, room + PACKET),
        [VMEM] * 4,
        [pltpu.VMEM((n_elem, 7 * LANES), BF16)],
        name="compact",
    )(mine, packets[0], packets[1], base)
    points = spread(gathered, "sub")
    received = exchange(packets, ("elem",))
    displacement, metric, state, traces, *packets = radial_call(
        points, node_ref, derivs, blending, base, state, minus, held_count, select, sent,
        coupling, link, received,
    )
    for sweep in range(1, ITERS):
        received = exchange(packets)
        base = call(local_body, shape_of(136, LANES), [VMEM] * 8, name="local")(
            state, traces, metric, const, minus, both, coupling, link
        )
        if sweep < ITERS - 1:
            state, traces, *packets = call(sweep_body, STATE, [VMEM] * 10, name="sweep")(
                base, held_count, select, sent, coupling, link, *received
            )
        else:
            solution_out = call(
                last_body,
                shape_of(5, 27, LANES),
                [VMEM] * 8,
                [pltpu.VMEM((136, LANES), F32)],
                held=False,
                name="last",
            )(base, held_count, coupling, link, *received)
    return displacement, solution_out


def solution(mesh):
    in_specs = (
        P(None, None, BOTH), P(None, BOTH), P(None, BOTH), P(BOTH), P(None, None, BOTH), P(None, None, BOTH),
        P(BOTH), P(None, BOTH), P(BOTH, None, None), P(), P(), P(),
    )
    out_specs = (P(None, None, BOTH), P(None, None, BOTH))
    return jax.shard_map(per_device, mesh=mesh, in_specs=in_specs, out_specs=out_specs, check_vma=False)
```

```python
import functools

import jax
import jax.numpy as jnp
import numpy as np
from jax import lax
from jax.experimental import pallas as pl
from jax.experimental.pallas import tpu as pltpu
from jax.sharding import PartitionSpec as P

ITERS = 3
BOTH = ("elem", "sub")
RADIUS = 1.5
FAR = 1000.0
LANES = 128
STRIP = 256
HEAD = 640
RUN = 768
PACKET = 384
TILES = 16
SLOTS = 8
INTERPRET = False
F32, BF16, I32 = jnp.float32, jnp.bfloat16, jnp.int32
VMEM = pltpu.MemorySpace.VMEM
HBM = pltpu.MemorySpace.HBM


def node_tables():
    slopes = np.array([[-1.5, 2.0, -0.5], [-0.5, 0.0, 0.5], [0.5, -2.0, 1.5]])
    one = np.eye(3)
    derivs = np.zeros((96, 32), np.float32)
    for axis, full in enumerate(
        (
            np.kron(one, np.kron(one, slopes)),
            np.kron(one, np.kron(slopes, one)),
            np.kron(slopes, np.eye(9)),
        )
    ):
        derivs[32 * axis : 32 * axis + 27, :27] = full
    blending = np.zeros((32, 8), np.float32)
    for node in range(27):
        place = (node % 3 - 1.0, node // 3 % 3 - 1.0, node // 9 - 1.0)
        for corner in range(8):
            weight = 1.0
            for axis in range(3):
                side = 1.0 if corner >> axis & 1 else -1.0
                weight *= (1.0 + side * place[axis]) / 2.0
            blending[node, corner] = weight
    select = np.zeros((288, 136), np.float32)
    for face in range(6):
        axis, layer = face // 2, 2 * (face % 2)
        nodes = [n for n in range(27) if n // 3**axis % 3 == layer]
        for var in range(5):
            for at, node in enumerate(nodes):
                select[48 * face + 9 * var + at, 27 * var + node] = 1.0
    place = np.zeros((270, 288), np.float32)
    for face in range(6):
        for entry in range(45):
            place[6 * entry + face, 48 * face + entry] = 1.0
    return derivs, blending, select, place


CORNERS = [2 * (c & 1) + 6 * (c >> 1 & 1) + 18 * (c >> 2) for c in range(8)]


def pieces(x, count):
    out = []
    for _ in range(count):
        piece = x.astype(BF16)
        out.append(piece)
        x = x - piece.astype(F32)
    return out


def stored_dot(a_ref, b):
    b1, b2 = pieces(b, 2)
    high = jnp.dot(a_ref[0], b1, preferred_element_type=F32)
    return high + (jnp.dot(a_ref[0], b2, preferred_element_type=F32) + jnp.dot(a_ref[1], b1, preferred_element_type=F32))


def split_dot(a, b):
    a1, a2 = pieces(a, 2)
    b1, b2 = pieces(b, 2)
    high = jnp.dot(a1, b1, preferred_element_type=F32)
    return high + (jnp.dot(a1, b2, preferred_element_type=F32) + jnp.dot(a2, b1, preferred_element_type=F32))


def pick_dot(a, b, count=2):
    out = None
    for piece in pieces(b, count):
        part = jnp.dot(a, piece, preferred_element_type=F32)
        out = part if out is None else out + part
    return out


def nt_dot(a, b):
    return lax.dot_general(a, b, (((1,), (1,)), ((), ())), preferred_element_type=F32)


def iota(shape, dim):
    return lax.broadcasted_iota(I32, shape, dim)


def flag(mask, dtype=F32):
    return jnp.where(mask, 1.0, 0.0).astype(dtype)


def call(body, out_shape, in_spaces, scratch=(), held=True, in_specs=None, out_specs=None, **kw):
    held = held if isinstance(held, list) else jax.tree.map(lambda _: held, out_shape)

    def place(s, stays):
        return pltpu.VMEM(s.shape, s.dtype) if stays and not INTERPRET else s

    run = pl.pallas_call(
        body,
        out_shape=jax.tree.map(place, out_shape, held),
        in_specs=in_specs or [pl.BlockSpec(memory_space=VMEM) for _ in in_spaces],
        out_specs=out_specs or jax.tree.map(lambda _: pl.BlockSpec(memory_space=VMEM), out_shape),
        scratch_shapes=list(scratch),
        interpret=INTERPRET,
        **kw,
    )

    def placed(*args):
        if INTERPRET:
            return run(*args)
        return run(*[a if s is None else pltpu.with_memory_space_constraint(a, s) for a, s in zip(args, in_spaces, strict=True)])

    return placed


def shape_of(*dims, dtype=F32):
    return jax.ShapeDtypeStruct(dims, dtype)


STATE = [shape_of(136, LANES), shape_of(6, 48, LANES), *[shape_of(24, LANES)] * 4]


def payload_body(count_ref, pos_ref, coef_ref, out_ref, row_ref):
    count = jnp.broadcast_to(count_ref[...], (1, LANES))[:, 0:32]
    live = iota((1, 32), 1) < count
    for axis in range(3):
        lanes = slice(32 * axis, 32 * axis + 32)
        row_ref[0:1, lanes] = jnp.where(live, pos_ref[axis : axis + 1, :], FAR)
        row_ref[1:2, lanes] = jnp.where(live, coef_ref[axis : axis + 1, :], 0.0)
    row_ref[0:1, 96:128] = jnp.zeros((1, 32), F32)
    row_ref[1:2, 96:128] = count.astype(F32)
    out_ref[...] = jnp.broadcast_to(row_ref[0:2, :][None], out_ref.shape)


def compact_body(in_ref, p0, p1, order_ref, out_ref, far_ref, part_ref):
    owners = in_ref.shape[0]
    copies, _, near = out_ref.shape
    near = near - PACKET
    me = lax.axis_index("sub")
    odd = me % 2 == 1
    ahead, back = jnp.where(odd, p1[...], p0[...]), jnp.where(odd, p0[...], p1[...])
    for peer in range(copies):
        for at in range(3):
            lanes = slice(near + LANES * at, near + LANES * at + LANES)
            rows = slice(8 * at, 8 * at + 8)
            out_ref[peer, :, lanes] = jnp.where(peer > me, ahead[rows], back[rows])
    first, second = in_ref[:, 0, :], in_ref[:, 1, :]
    wide = jnp.broadcast_to(second[:, 96:97], (owners, LANES))
    below = flag(iota((owners, owners), 1) < iota((owners, owners), 0), BF16)
    above = flag(iota((owners, owners), 0) < iota((owners, owners), 1), BF16)
    start_col = jnp.dot(below, wide.astype(BF16), preferred_element_type=F32)
    pick = flag(iota((8, LANES), 1) == 96, BF16)
    count_row = nt_dot(pick, second.astype(BF16))
    start_row = jnp.dot(count_row.astype(BF16), above, preferred_element_type=F32)
    low, end = start_row[0:1, :], (start_row + count_row)[0:1, :]
    total = jnp.max(end, axis=1, keepdims=True)
    for at, piece in enumerate(pieces(first, 3)):
        part_ref[:, LANES * at : LANES * at + LANES] = piece
    for at, piece in enumerate(pieces(second, 2) + pieces(start_col, 2)):
        part_ref[:, LANES * (3 + at) : LANES * (4 + at)] = piece
    feature, group = iota((8, LANES), 0), iota((8, LANES), 1) // 32
    fold_first = flag((feature < 3) & (feature == group), BF16)
    fold_second = flag((feature > 3) & (feature < 7) & (feature == group + 4), BF16)

    def one_strip(base, strip, target, at):
        slot = (iota((strip, LANES), 1) % 32).astype(F32)
        place = (iota((strip, owners), 0) + base).astype(F32)
        owner = flag((place >= low) & (place < end), BF16)
        found = jnp.dot(owner, part_ref[...], preferred_element_type=F32)
        start = found[:, 5 * LANES : 6 * LANES] + found[:, 6 * LANES :]
        here = (iota((strip, LANES), 0) + base).astype(F32)
        mine = slot == here - start
        out = None
        for k in range(3):
            a = jnp.where(mine, found[:, LANES * k : LANES * k + LANES], 0.0).astype(BF16)
            both = nt_dot(fold_first, a)
            if k < 2:
                b = jnp.where(mine, found[:, LANES * (3 + k) : LANES * (4 + k)], 0.0).astype(BF16)
                both = both + nt_dot(fold_second, b)
            out = both if out is None else out + both
        dead = (iota((8, strip), 1) + base).astype(F32) >= total
        row = iota((8, strip), 0)
        out = jnp.where(dead, jnp.where(row < 3, FAR, 0.0), out)
        square = jnp.sum(jnp.where(row < 3, out * out, 0.0), axis=0, keepdims=True)
        out = jnp.where(row == 3, square, out)
        out = jnp.where(row == 7, total, out)
        target[:, :, at : at + strip] = jnp.broadcast_to(out[None], (copies, 8, strip))

    head = min(HEAD, near)
    one_strip(0, head, out_ref, 0)
    if head < near or far_ref is not None:
        count = jnp.max(total)
    if head < near:

        @pl.when(count > head)
        def second():
            one_strip(head, near - head, out_ref, head)

    if far_ref is not None:
        for at in range(0, far_ref.shape[2], STRIP):

            @pl.when(count > near + at)
            def further(at=at):
                one_strip(near + at, min(STRIP, far_ref.shape[2] - at), far_ref, at)


def radial_displacement(z_ref, far_ref, node_ref, corner_ref, hit_ref, rank_ref, list_ref, sum_ref, over_ref, over_smem, sem):
    groups, _, run = z_ref.shape
    run = run - PACKET
    blocks = run // LANES
    at = [[node_ref[i, k : k + 1, :] for k in CORNERS] for i in range(3)]
    middle, reach = [], [None] * 8
    for i in range(3):
        low = functools.reduce(jnp.minimum, at[i])
        high = functools.reduce(jnp.maximum, at[i])
        middle.append(0.5 * (low + high))
        for c in range(8):
            gap = (at[i][c] - middle[i]) ** 2
            reach[c] = gap if i == 0 else reach[c] + gap
    limit = RADIUS + jnp.sqrt(functools.reduce(jnp.maximum, reach))
    offset = middle[0] ** 2 + middle[1] ** 2 + middle[2] ** 2 - limit * limit * 1.001 - 0.2
    row = iota((LANES, LANES), 0)
    table = jnp.where((row == 3) | (row == 11), 1.0, 0.0)
    for i in range(3):
        high, low = (p.astype(F32) for p in pieces(-2.0 * middle[i], 2))
        table = jnp.where((row == i) | (row == 8 + i), high, jnp.where(row == 16 + i, low, table))
    probe = jnp.transpose(table)[:, 0:24].astype(BF16)
    offset = jnp.transpose(jnp.broadcast_to(offset, (LANES, LANES)))
    offset = jnp.concatenate([offset] * blocks, axis=1)
    pick = iota((8, LANES), 0) * TILES + iota((8, LANES), 1) % TILES
    for i in range(3):
        for c in range(8):
            corner_ref[i, 8 * c : 8 * c + 8, :] = jnp.take_along_axis(
                jnp.broadcast_to(at[i][c], (8, LANES)), pick, axis=1
            ) * (1.0 / RADIUS)
        sum_ref[i] = jnp.zeros((64, LANES), F32)
    counts = [jnp.max(z_ref[g, 7:8, 0:LANES]).astype(I32) for g in range(groups)]
    most = functools.reduce(jnp.maximum, counts)
    source, target = iota((LANES, 2 * LANES), 0), iota((LANES, 2 * LANES), 1)
    same_half = source // 64 == target // 64
    prefix = flag(
        (target < LANES) & same_half & (source <= target)
        | (target >= LANES) & (source // 64 == target - LANES),
        BF16,
    )
    half = iota((TILES, LANES), 1) // 64

    def extract(source, g, start, block, shift):
        points = source[g, :, pl.ds(pl.multiple_of(start + block * LANES, LANES), LANES)]
        three = jnp.concatenate([p.astype(F32) for p in pieces(points, 3)], axis=0).astype(BF16)
        rank = rank_ref[pl.ds(pl.multiple_of((g * blocks + block) * TILES, TILES), TILES), :]
        entries = []
        for h in range(2):
            key = jnp.where(half == h, rank - shift, 0.0)
            chosen = jnp.concatenate([flag(key == s + 1.0) for s in range(SLOTS)], axis=0).astype(BF16)
            found = nt_dot(three, chosen)
            found = found[0:8] + found[8:16] + found[16:24]
            entries.append(jnp.where(iota((8, LANES), 0) < 4, found * (1.0 / RADIUS), found * 4.0))
        return entries

    def one_part(source, first, start, ahead):
        for g in range(groups):
            points = source[g, :, pl.ds(pl.multiple_of(start, LANES), run)]
            high, low = pieces(points, 2)
            both = jnp.concatenate([high.astype(F32), low.astype(F32), high.astype(F32)], axis=0)
            gap = jnp.dot(probe, both.astype(BF16), preferred_element_type=F32) + offset
            best = gap[0:TILES]
            for e in range(1, 8):
                best = jnp.minimum(best, gap[TILES * e : TILES * e + TILES])
            lane = iota((TILES, run), 1) + (ahead + start)
            hit = flag((best <= 0.0) & (lane >= first) & (lane < counts[g]))
            for b in range(blocks):
                hit_ref[(g * blocks + b) * TILES : (g * blocks + b + 1) * TILES, :] = hit[:, LANES * b : LANES * b + LANES]
        hits = hit_ref[...]
        ranks = jnp.dot(hits.astype(BF16), prefix, preferred_element_type=F32)
        rank_ref[...] = jnp.where(hits > 0.0, ranks[:, 0:LANES], -1000.0)
        filled = ranks[:, LANES:].reshape(groups * blocks, TILES, LANES)
        filled = jnp.max(filled, axis=1).astype(I32)
        over_ref[...] = filled
        copy = pltpu.make_async_copy(over_ref, over_smem, sem)
        copy.start()
        length = jnp.int32(0)
        for g in range(groups):
            inside = jnp.clip(counts[g] - (ahead + start), 0, run)
            for b in range(blocks):
                one, two = extract(source, g, start, b, 0.0)
                list_ref[length] = one
                length = length + jnp.where(inside > LANES * b, 1, 0)
                list_ref[length] = two
                length = length + jnp.where(inside > LANES * b + 64, 1, 0)
        def more(length):
            def block_more(index, length):
                g, b = index // blocks, index % blocks

                def round_more(r, length):
                    one, two = extract(source, g, start, b, (r * SLOTS).astype(F32))
                    list_ref[length] = one
                    length = length + jnp.where(over_smem[index, 0] > r * SLOTS, 1, 0)
                    list_ref[length] = two
                    length = length + jnp.where(over_smem[index, 1] > r * SLOTS, 1, 0)
                    return length

                rounds = (jnp.maximum(over_smem[index, 0], over_smem[index, 1]) + SLOTS - 1) // SLOTS
                return lax.fori_loop(1, rounds, round_more, length)

            for g in range(groups):
                crowd = [over_smem[g * blocks + b, h] for b in range(blocks) for h in range(2)]
                last = jnp.where(functools.reduce(jnp.maximum, crowd) > SLOTS, blocks, 0)
                length = lax.fori_loop(g * blocks, g * blocks + last, block_more, length)
            return length

        def four(step, carry):
            for i in range(2):
                for c in range(0, 64, 8):
                    total = [sum_ref[axis, c : c + 8, :] for axis in range(3)]
                    place = [corner_ref[axis, c : c + 8, :] for axis in range(3)]
                    for e in range(2):
                        entry = list_ref.at[4 * step + 2 * i + e]
                        gap = [place[axis] - entry[axis : axis + 1, :] for axis in range(3)]
                        square = gap[0] * gap[0] + gap[1] * gap[1] + gap[2] * gap[2]
                        ratio = square * lax.rsqrt(jnp.maximum(square, 1e-20))
                        inside = jnp.maximum(1.0 - ratio, 0.0)
                        inside = inside * inside
                        kernel = inside * inside * (ratio + 0.25)
                        for axis in range(3):
                            total[axis] = total[axis] + entry[4 + axis : 5 + axis, :] * kernel
                    for axis in range(3):
                        sum_ref[axis, c : c + 8, :] = total[axis]
            return carry

        def evaluate(length):
            for e in range(4):
                list_ref[length + e] = jnp.zeros((8, LANES), F32)
            lax.fori_loop(0, (length + 3) // 4, four, 0)

        evaluate(length)
        copy.wait()

        @pl.when(jnp.max(filled) > SLOTS)
        def crowded():
            evaluate(more(jnp.int32(0)))

    one_part(z_ref, 0, 0, 0)
    if far_ref is not None:
        step = min(run, far_ref.shape[2])

        def far_part(part, carry):
            first = (part - 1) * step
            one_part(far_ref, run + first, jnp.minimum(first, far_ref.shape[2] - step), run)
            return carry

        lax.fori_loop(1, 1 + (jnp.maximum(most - run, 0) + (step - 1)) // step, far_part, 0)
    spread = flag(iota((LANES, LANES), 0) % TILES == iota((LANES, LANES), 1) % TILES, BF16)
    own = iota((8, LANES), 0) == iota((8, LANES), 1) // TILES
    out = []
    for i in range(3):
        total = None
        for piece in pieces(sum_ref[i], 2):
            part = jnp.dot(piece, spread, preferred_element_type=F32)
            total = part if total is None else total + part
        rows = [
            jnp.sum(jnp.where(own, total[8 * c : 8 * c + 8], 0.0), axis=0, keepdims=True) for c in range(8)
        ]
        out.append(jnp.concatenate(rows, axis=0))
    return out


def radial_body(
    z_ref, far_ref, node_any, derivs_any, blend_any, base_ref, start_ref, minus_inv_ref, count_ref, select_any, send_ref,
    m_ref, where_ref, elem_0, elem_1,
    disp_ref, metric_ref, state_ref, trace_ref, p0, p1, p2, p3,
    corner_ref, hit_ref, rank_ref, list_ref, sum_ref, over_ref, over_smem, sem, nodes_ref, shift_ref, out_sem, node_ref, derivs_ref, blend_ref, select_ref, in_sems,
):
    moves = ((node_any, node_ref), (blend_any, blend_ref), (derivs_any, derivs_ref), (select_any, select_ref))
    copies = [pltpu.make_async_copy(a, b, in_sems.at[k]) for k, (a, b) in enumerate(moves)]
    for copy in copies:
        copy.start()
    packet_refs = (p0, p1, p2, p3)
    me, last = lax.axis_index("sub"), z_ref.shape[0] - 1
    sides = []
    for step in (-1, 1):
        peer, there = jnp.clip(me + step, 0, last), (me + step >= 0) & (me + step <= last)
        rows = [z_ref[peer, :, z_ref.shape[2] - PACKET + LANES * at :][:, 0:LANES] for at in range(3)]
        sides.append(jnp.where(there, jnp.concatenate(rows, axis=0), 0.0))
    base = base_ref[...] + from_neighbours(*sides, *in_line("elem", elem_0[...], elem_1[...]), where_ref, m_ref)
    copies[0].wait()
    corner = radial_displacement(
        z_ref, far_ref, node_ref, corner_ref, hit_ref, rank_ref, list_ref, sum_ref, over_ref, over_smem, sem
    )
    for copy in copies[1:]:
        copy.wait()
    nodes_ref[...] = jnp.zeros_like(nodes_ref)
    for i in range(3):
        shift = pick_dot(blend_ref[...], corner[i], 2)
        shift_ref[i] = shift[0:27]
        nodes_ref[0:27, LANES * i : LANES * i + LANES] = node_ref[i] + shift[0:27]
    out = pltpu.make_async_copy(shift_ref, disp_ref, out_sem)
    out.start()
    jac = pick_dot(derivs_ref[...], nodes_ref[...], 3)
    j = [[jac[32 * l : 32 * l + 32, LANES * i : LANES * i + LANES] for l in range(3)] for i in range(3)]
    minor_a = j[1][1] * j[2][2] - j[1][2] * j[2][1]
    minor_b = j[1][0] * j[2][2] - j[1][2] * j[2][0]
    minor_c = j[1][0] * j[2][1] - j[1][1] * j[2][0]
    metric = 8.0 * (j[0][0] * minor_a - j[0][1] * minor_b + j[0][2] * minor_c)
    metric_ref[...] = jnp.zeros_like(metric_ref)
    for v in range(5):
        metric_ref[27 * v : 27 * v + 27, :] = metric[0:27]
    state = base + stored_dot(minus_inv_ref, metric_ref[...] * start_ref[...])
    finish(state, count_ref, select_ref, send_ref, state_ref, trace_ref, packet_refs)
    out.wait()


def finish(state, count_ref, select_ref, send_ref, state_ref, trace_ref, packet_refs):
    state = jnp.where(iota(state.shape, 1) < jnp.broadcast_to(count_ref[...], state.shape), state, 0.0)
    state_ref[...] = state
    traces = pick_dot(select_ref[...], state, 2)
    for f in range(6):
        trace_ref[f] = traces[48 * f : 48 * f + 48]
    tiles = [traces[48 * f : 48 * f + 48] for f in range(6)]
    left = iota((24, LANES), 1) < 64
    for pair in range(2):
        both = gather_columns(tiles, send_ref[pair : pair + 1, :], 0)
        top, bottom = both[0:24], both[24:48]
        ahead = jnp.where(left, top, pltpu.roll(bottom, 64, 1))
        back = jnp.where(left, pltpu.roll(top, 64, 1), bottom)
        odd = lax.axis_index(("sub", "elem")[pair]) % 2 == 1
        packet_refs[2 * pair][...] = jnp.where(odd, back, ahead)
        packet_refs[2 * pair + 1][...] = jnp.where(odd, ahead, back)


def gather_columns(tiles, index, first):
    rows = tiles[0].shape[0]
    tile = jnp.broadcast_to(index // LANES - first, (rows, LANES))
    lane = jnp.broadcast_to(index % LANES, (rows, LANES))
    out = jnp.zeros((rows, LANES), F32)
    for t, values in enumerate(tiles):
        out = jnp.where(tile == t, jnp.take_along_axis(values, lane, axis=1), out)
    return out


def in_line(axis, first, second):
    odd = lax.axis_index(axis) % 2 == 1
    return jnp.where(odd, first, second), jnp.where(odd, second, first)


def from_neighbours(before_sub, behind_sub, before_elem, behind_elem, where_ref, m_ref):
    packets = (before_sub, behind_sub, before_elem, behind_elem)
    columns = []
    for f in range(6):
        index = where_ref[f : f + 1, :] - 6 * LANES
        packet = jnp.broadcast_to(jnp.where(index >= 0, index // 64, -1), (24, LANES))
        lane = jnp.broadcast_to(index % 64, (24, LANES))
        halves = []
        for half in range(2):
            found = jnp.zeros((24, LANES), F32)
            for q, values in enumerate(packets):
                found = jnp.where(packet == q, jnp.take_along_axis(values, lane + 64 * half, axis=1), found)
            halves.append(found)
        columns += halves
    return stored_dot(m_ref, jnp.concatenate(columns, axis=0))


def arrived(sub_0, sub_1, elem_0, elem_1, where_ref, m_ref):
    sub = in_line("sub", sub_0[...], sub_1[...])
    return from_neighbours(*sub, *in_line("elem", elem_0[...], elem_1[...]), where_ref, m_ref)


def setup_body(
    u_ref, count_ref, select_ref, send_ref, vol_ref, inv_ref, lift_ref, place_ref, right_ref, where_ref,
    state_ref, trace_ref, p0, p1, p2, p3, held_ref, sent_ref, link_ref, minus_ref, both_ref, m_ref, const_ref, base_ref,
    flat_ref, wide_ref,
):
    held_ref[...] = jnp.broadcast_to(count_ref[...], held_ref.shape)
    for q in range(4):
        sent_ref[q // 2 : q // 2 + 1, 64 * (q % 2) : 64 * (q % 2) + 64] = send_ref[0, q : q + 1, :]
    link_ref[...] = where_ref[...]
    flat_ref[...] = jnp.zeros_like(flat_ref)
    for v in range(5):
        flat_ref[27 * v : 27 * v + 27, :] = u_ref[v]
    finish(flat_ref[...], held_ref, select_ref, sent_ref, state_ref, trace_ref, (p0, p1, p2, p3))
    wide_ref[...] = jnp.zeros_like(wide_ref)
    wide_ref[0:135, 0:135] = inv_ref[...]
    inverse = wide_ref[:, 0:136]
    wide_ref[0:135, 0:135] = -split_dot(inv_ref[...], vol_ref[...])
    for k, piece in enumerate(pieces(-inverse, 2)):
        minus_ref[k] = piece
    for k, piece in enumerate(pieces(wide_ref[:, 0:136], 2)):
        both_ref[k] = piece
    coupling = split_dot(inverse[:, 0:135], lift_ref[...])
    moved = [jnp.dot(piece, place_ref[...], preferred_element_type=F32) for piece in pieces(coupling, 2)]
    for k in range(2):
        m_ref[k] = moved[k].astype(BF16)
    flat_ref[...] = jnp.zeros_like(flat_ref)
    for v in range(5):
        flat_ref[27 * v : 27 * v + 27, :] = right_ref[v]
    const = split_dot(inverse, flat_ref[...])
    const_ref[...] = const
    state = state_ref[...]
    base_ref[...] = state + const + stored_dot(both_ref, state) + local_part(trace_ref, where_ref, m_ref)


def local_part(trace_ref, where_ref, m_ref):
    tiles = [trace_ref[f] for f in range(6)]
    columns = [gather_columns(tiles, where_ref[f : f + 1, :], 0) for f in range(6)]
    return stored_dot(m_ref, jnp.concatenate(columns, axis=0))


def local_body(state_ref, trace_ref, metric_ref, const_ref, minus_ref, both_ref, m_ref, where_ref, out_ref):
    state = state_ref[...]
    out = state + const_ref[...] + stored_dot(both_ref, state)
    out = out + stored_dot(minus_ref, metric_ref[...] * state)
    out_ref[...] = out + local_part(trace_ref, where_ref, m_ref)


def sweep_body(
    base_ref, count_ref, select_ref, send_ref, m_ref, where_ref, sub_0, sub_1, elem_0, elem_1,
    state_ref, trace_ref, p0, p1, p2, p3,
):
    packet_refs = (p0, p1, p2, p3)
    state = base_ref[...] + arrived(sub_0, sub_1, elem_0, elem_1, where_ref, m_ref)
    finish(state, count_ref, select_ref, send_ref, state_ref, trace_ref, packet_refs)


def last_body(base_ref, count_ref, m_ref, where_ref, sub_0, sub_1, elem_0, elem_1, out_ref, state_ref):
    state = base_ref[...] + arrived(sub_0, sub_1, elem_0, elem_1, where_ref, m_ref)
    state_ref[...] = jnp.where(iota(state.shape, 1) < jnp.broadcast_to(count_ref[...], state.shape), state, 0.0)
    for v in range(5):
        out_ref[v] = state_ref[27 * v : 27 * v + 27, :]


def exchange(packets, axes=("sub", "elem")):
    out = []
    for axis in axes:
        first = 0 if axis == "sub" else 2
        size = lax.axis_size(axis)
        for turn in range(2):
            partner = [(i ^ 1) if turn == 0 else ((i + 1) ^ 1) - 1 for i in range(size)]
            pairs = [(i, j) for i, j in enumerate(partner) if 0 <= j < size]
            out.append(lax.ppermute(packets[first + turn], axis, pairs))
    return out


def spread(copies, axis):
    return lax.all_to_all(copies, axis, split_axis=0, concat_axis=0, tiled=True)


def radial_call(points, far, node_ref, derivs, blending, base, state, minus, elem_count, select, send, coupling, face_link, received):
    groups, _, run = points.shape
    blocks = (run - PACKET) // LANES * groups
    return call(
        radial_body,
        [shape_of(3, 27, LANES), shape_of(136, LANES), *STATE],
        [VMEM, VMEM, None, None, None, VMEM, VMEM, VMEM, VMEM, None, VMEM, VMEM, VMEM, VMEM, VMEM],
        [
            pltpu.VMEM((3, 64, LANES), F32),
            pltpu.VMEM((blocks * TILES, LANES), F32),
            pltpu.VMEM((blocks * TILES, LANES), F32),
            pltpu.VMEM((blocks * 16 + 8, 8, LANES), F32),
            pltpu.VMEM((3, 64, LANES), F32),
            pltpu.VMEM((blocks, LANES), I32),
            pltpu.SMEM((blocks, LANES), I32),
            pltpu.SemaphoreType.DMA,
            pltpu.VMEM((32, 3 * LANES), F32),
            pltpu.VMEM((3, 27, LANES), F32),
            pltpu.SemaphoreType.DMA,
            pltpu.VMEM(node_ref.shape, F32),
            pltpu.VMEM(derivs.shape, BF16),
            pltpu.VMEM(blending.shape, BF16),
            pltpu.VMEM(select.shape, BF16),
            pltpu.SemaphoreType.DMA((4,)),
        ],
        in_specs=[pl.BlockSpec(memory_space=pl.ANY if k in (2, 3, 4, 9) else VMEM) for k in range(15)],
        held=[False] + [True] * 7,
        out_specs=[pl.BlockSpec(memory_space=pl.ANY)] + [pl.BlockSpec(memory_space=VMEM)] * 7,
        name="radial",
    )(
        points, far, node_ref, derivs, blending, base, state, minus, elem_count, select, send,
        coupling, face_link, *received,
    )


def per_device(
    node_ref, cp_pos, cp_coef, cp_count, u_prev, right_side, elem_count, face_link, send_list,
    vol_block, block_inv, lift_matrix,
):
    derivs, blending, select, place = node_tables()
    derivs, blending = jnp.asarray(derivs, BF16), jnp.asarray(blending, BF16)
    select, place = jnp.asarray(select, BF16), jnp.asarray(place, BF16)
    n_elem, n_sub = lax.axis_size("elem"), lax.axis_size("sub")
    room = n_elem * cp_pos.shape[1]

    copies = call(
        payload_body, shape_of(n_elem, 2, LANES), [None] * 3, [pltpu.VMEM((8, LANES), F32)], name="payload"
    )(cp_count.reshape(1, 1), cp_pos, cp_coef)
    mine = spread(copies, "elem")
    *first, held_count, sent, link, minus, both, coupling, const, base = call(
        setup_body,
        [
            *STATE, shape_of(1, LANES, dtype=I32), shape_of(2, LANES, dtype=I32), shape_of(6, LANES, dtype=I32),
            shape_of(2, 136, 136, dtype=BF16), shape_of(2, 136, 136, dtype=BF16), shape_of(2, 136, 288, dtype=BF16),
            shape_of(136, LANES), shape_of(136, LANES),
        ],
        [None, None, HBM, None, HBM, HBM, HBM, HBM, HBM, HBM],
        [pltpu.VMEM((136, LANES), F32), pltpu.VMEM((136, 256), F32)],
        name="setup",
    )(
        u_prev, elem_count.reshape(1, 1), select, send_list, vol_block, block_inv, lift_matrix, place, right_side, face_link
    )
    state, traces, *packets = first
    near = min(RUN, room)
    gathered, rest = call(
        compact_body,
        [shape_of(n_sub, 8, near + PACKET), shape_of(n_sub, 8, max(room - near, near))],
        [VMEM] * 4,
        [pltpu.VMEM((n_elem, 7 * LANES), BF16)],
        name="compact",
    )(mine, packets[0], packets[1], base)
    points = spread(gathered, "sub")
    received = exchange(packets, ("elem",))
    far = lax.cond(jnp.max(points[:, 7, 0]) > near, lambda x: spread(x, "sub"), lambda x: x, rest)
    displacement, metric, state, traces, *packets = radial_call(
        points, far, node_ref, derivs, blending, base, state, minus, held_count, select, sent,
        coupling, link, received,
    )
    for sweep in range(1, ITERS):
        received = exchange(packets)
        base = call(local_body, shape_of(136, LANES), [VMEM] * 8, name="local")(
            state, traces, metric, const, minus, both, coupling, link
        )
        if sweep < ITERS - 1:
            state, traces, *packets = call(sweep_body, STATE, [VMEM] * 10, name="sweep")(
                base, held_count, select, sent, coupling, link, *received
            )
        else:
            solution_out = call(
                last_body,
                shape_of(5, 27, LANES),
                [VMEM] * 8,
                [pltpu.VMEM((136, LANES), F32)],
                held=False,
                name="last",
            )(base, held_count, coupling, link, *received)
    return displacement, solution_out


def solution(mesh):
    in_specs = (
        P(None, None, BOTH), P(None, BOTH), P(None, BOTH), P(BOTH), P(None, None, BOTH), P(None, None, BOTH),
        P(BOTH), P(None, BOTH), P(BOTH, None, None), P(), P(), P(),
    )
    out_specs = (P(None, None, BOTH), P(None, None, BOTH))
    return jax.shard_map(per_device, mesh=mesh, in_specs=in_specs, out_specs=out_specs, check_vma=False)
```

```python
import functools

import jax
import jax.numpy as jnp
import numpy as np
from jax import lax
from jax.experimental import pallas as pl
from jax.experimental.pallas import tpu as pltpu
from jax.sharding import PartitionSpec as P

ITERS = 3
BOTH = ("elem", "sub")
RADIUS = 1.5
FAR = 1000.0
LANES = 128
STRIP = 256
HEAD = 640
RUN = 768
PACKET = 384
TILES = 16
SLOTS = 8
INTERPRET = False
F32, BF16, I32 = jnp.float32, jnp.bfloat16, jnp.int32
VMEM = pltpu.MemorySpace.VMEM
HBM = pltpu.MemorySpace.HBM


def node_tables():
    slopes = np.array([[-1.5, 2.0, -0.5], [-0.5, 0.0, 0.5], [0.5, -2.0, 1.5]])
    one = np.eye(3)
    derivs = np.zeros((96, 32), np.float32)
    for axis, full in enumerate(
        (
            np.kron(one, np.kron(one, slopes)),
            np.kron(one, np.kron(slopes, one)),
            np.kron(slopes, np.eye(9)),
        )
    ):
        derivs[32 * axis : 32 * axis + 27, :27] = full
    blending = np.zeros((32, 8), np.float32)
    for node in range(27):
        place = (node % 3 - 1.0, node // 3 % 3 - 1.0, node // 9 - 1.0)
        for corner in range(8):
            weight = 1.0
            for axis in range(3):
                side = 1.0 if corner >> axis & 1 else -1.0
                weight *= (1.0 + side * place[axis]) / 2.0
            blending[node, corner] = weight
    select = np.zeros((288, 136), np.float32)
    for face in range(6):
        axis, layer = face // 2, 2 * (face % 2)
        nodes = [n for n in range(27) if n // 3**axis % 3 == layer]
        for var in range(5):
            for at, node in enumerate(nodes):
                select[48 * face + 9 * var + at, 27 * var + node] = 1.0
    place = np.zeros((270, 288), np.float32)
    for face in range(6):
        for entry in range(45):
            place[6 * entry + face, 48 * face + entry] = 1.0
    return derivs, blending, select, place


CORNERS = [2 * (c & 1) + 6 * (c >> 1 & 1) + 18 * (c >> 2) for c in range(8)]


def pieces(x, count):
    out = []
    for _ in range(count):
        piece = x.astype(BF16)
        out.append(piece)
        x = x - piece.astype(F32)
    return out


def stored_dot(a_ref, b):
    b1, b2 = pieces(b, 2)
    high = jnp.dot(a_ref[0], b1, preferred_element_type=F32)
    return high + (jnp.dot(a_ref[0], b2, preferred_element_type=F32) + jnp.dot(a_ref[1], b1, preferred_element_type=F32))


def split_dot(a, b):
    a1, a2 = pieces(a, 2)
    b1, b2 = pieces(b, 2)
    high = jnp.dot(a1, b1, preferred_element_type=F32)
    return high + (jnp.dot(a1, b2, preferred_element_type=F32) + jnp.dot(a2, b1, preferred_element_type=F32))


def pick_dot(a, b, count=2):
    out = None
    for piece in pieces(b, count):
        part = jnp.dot(a, piece, preferred_element_type=F32)
        out = part if out is None else out + part
    return out


def nt_dot(a, b):
    return lax.dot_general(a, b, (((1,), (1,)), ((), ())), preferred_element_type=F32)


def iota(shape, dim):
    return lax.broadcasted_iota(I32, shape, dim)


def flag(mask, dtype=F32):
    return jnp.where(mask, 1.0, 0.0).astype(dtype)


def call(body, out_shape, in_spaces, scratch=(), held=True, in_specs=None, out_specs=None, **kw):
    held = held if isinstance(held, list) else jax.tree.map(lambda _: held, out_shape)

    def place(s, stays):
        return pltpu.VMEM(s.shape, s.dtype) if stays and not INTERPRET else s

    run = pl.pallas_call(
        body,
        out_shape=jax.tree.map(place, out_shape, held),
        in_specs=in_specs or [pl.BlockSpec(memory_space=VMEM) for _ in in_spaces],
        out_specs=out_specs or jax.tree.map(lambda _: pl.BlockSpec(memory_space=VMEM), out_shape),
        scratch_shapes=list(scratch),
        interpret=INTERPRET,
        **kw,
    )

    def placed(*args):
        if INTERPRET:
            return run(*args)
        return run(*[a if s is None else pltpu.with_memory_space_constraint(a, s) for a, s in zip(args, in_spaces, strict=True)])

    return placed


def shape_of(*dims, dtype=F32):
    return jax.ShapeDtypeStruct(dims, dtype)


STATE = [shape_of(136, LANES), shape_of(6, 48, LANES), *[shape_of(24, LANES)] * 4]


def payload_body(count_ref, pos_ref, coef_ref, out_ref, row_ref):
    count = jnp.broadcast_to(count_ref[...], (1, LANES))[:, 0:32]
    live = iota((1, 32), 1) < count
    for axis in range(3):
        lanes = slice(32 * axis, 32 * axis + 32)
        row_ref[0:1, lanes] = jnp.where(live, pos_ref[axis : axis + 1, :], FAR)
        row_ref[1:2, lanes] = jnp.where(live, coef_ref[axis : axis + 1, :], 0.0)
    row_ref[0:1, 96:128] = jnp.zeros((1, 32), F32)
    row_ref[1:2, 96:128] = count.astype(F32)
    out_ref[...] = jnp.broadcast_to(row_ref[0:2, :][None], out_ref.shape)


def compact_body(in_ref, p0, p1, order_ref, out_ref, far_ref, part_ref):
    owners = in_ref.shape[0]
    copies, _, near = out_ref.shape
    near = near - PACKET
    me = lax.axis_index("sub")
    odd = me % 2 == 1
    ahead, back = jnp.where(odd, p1[...], p0[...]), jnp.where(odd, p0[...], p1[...])
    for peer in range(copies):
        for at in range(3):
            lanes = slice(near + LANES * at, near + LANES * at + LANES)
            rows = slice(8 * at, 8 * at + 8)
            out_ref[peer, :, lanes] = jnp.where(peer > me, ahead[rows], back[rows])
    first, second = in_ref[:, 0, :], in_ref[:, 1, :]
    wide = jnp.broadcast_to(second[:, 96:97], (owners, LANES))
    below = flag(iota((owners, owners), 1) < iota((owners, owners), 0), BF16)
    above = flag(iota((owners, owners), 0) < iota((owners, owners), 1), BF16)
    start_col = jnp.dot(below, wide.astype(BF16), preferred_element_type=F32)
    pick = flag(iota((8, LANES), 1) == 96, BF16)
    count_row = nt_dot(pick, second.astype(BF16))
    start_row = jnp.dot(count_row.astype(BF16), above, preferred_element_type=F32)
    low, end = start_row[0:1, :], (start_row + count_row)[0:1, :]
    total = jnp.max(end, axis=1, keepdims=True)
    for at, piece in enumerate(pieces(first, 3)):
        part_ref[:, LANES * at : LANES * at + LANES] = piece
    for at, piece in enumerate(pieces(second, 2) + pieces(start_col, 2)):
        part_ref[:, LANES * (3 + at) : LANES * (4 + at)] = piece
    feature, group = iota((8, LANES), 0), iota((8, LANES), 1) // 32
    fold_first = flag((feature < 3) & (feature == group), BF16)
    fold_second = flag((feature > 3) & (feature < 7) & (feature == group + 4), BF16)

    def one_strip(base, strip, target, at):
        slot = (iota((strip, LANES), 1) % 32).astype(F32)
        place = (iota((strip, owners), 0) + base).astype(F32)
        owner = flag((place >= low) & (place < end), BF16)
        found = jnp.dot(owner, part_ref[...], preferred_element_type=F32)
        start = found[:, 5 * LANES : 6 * LANES] + found[:, 6 * LANES :]
        here = (iota((strip, LANES), 0) + base).astype(F32)
        mine = slot == here - start
        out = None
        for k in range(3):
            a = jnp.where(mine, found[:, LANES * k : LANES * k + LANES], 0.0).astype(BF16)
            both = nt_dot(fold_first, a)
            if k < 2:
                b = jnp.where(mine, found[:, LANES * (3 + k) : LANES * (4 + k)], 0.0).astype(BF16)
                both = both + nt_dot(fold_second, b)
            out = both if out is None else out + both
        dead = (iota((8, strip), 1) + base).astype(F32) >= total
        row = iota((8, strip), 0)
        out = jnp.where(dead, jnp.where(row < 3, FAR, 0.0), out)
        square = jnp.sum(jnp.where(row < 3, out * out, 0.0), axis=0, keepdims=True)
        out = jnp.where(row == 3, square, out)
        out = jnp.where(row == 7, total, out)
        target[:, :, at : at + strip] = jnp.broadcast_to(out[None], (copies, 8, strip))

    head = min(HEAD, near)
    one_strip(0, head, out_ref, 0)
    if head < near or far_ref is not None:
        count = jnp.max(total)
    if head < near:

        @pl.when(count > head)
        def second():
            one_strip(head, near - head, out_ref, head)

    if far_ref is not None:
        for at in range(0, far_ref.shape[2], STRIP):

            @pl.when(count > near + at)
            def further(at=at):
                one_strip(near + at, min(STRIP, far_ref.shape[2] - at), far_ref, at)


def radial_displacement(z_ref, far_ref, node_ref, corner_ref, hit_ref, rank_ref, list_ref, sum_ref, over_ref, over_smem, sem):
    groups, _, run = z_ref.shape
    run = run - PACKET
    blocks = run // LANES
    at = [[node_ref[i, k : k + 1, :] for k in CORNERS] for i in range(3)]
    middle, reach = [], [None] * 8
    for i in range(3):
        low = functools.reduce(jnp.minimum, at[i])
        high = functools.reduce(jnp.maximum, at[i])
        middle.append(0.5 * (low + high))
        for c in range(8):
            gap = (at[i][c] - middle[i]) ** 2
            reach[c] = gap if i == 0 else reach[c] + gap
    limit = RADIUS + jnp.sqrt(functools.reduce(jnp.maximum, reach))
    offset = middle[0] ** 2 + middle[1] ** 2 + middle[2] ** 2 - limit * limit * 1.001 - 0.2
    row = iota((LANES, LANES), 0)
    table = jnp.where((row == 3) | (row == 11), 1.0, 0.0)
    for i in range(3):
        high, low = (p.astype(F32) for p in pieces(-2.0 * middle[i], 2))
        table = jnp.where((row == i) | (row == 8 + i), high, jnp.where(row == 16 + i, low, table))
    probe = jnp.transpose(table)[:, 0:24].astype(BF16)
    offset = jnp.transpose(jnp.broadcast_to(offset, (LANES, LANES)))
    offset = jnp.concatenate([offset] * blocks, axis=1)
    pick = iota((8, LANES), 0) * TILES + iota((8, LANES), 1) % TILES
    for i in range(3):
        for c in range(8):
            corner_ref[i, 8 * c : 8 * c + 8, :] = jnp.take_along_axis(
                jnp.broadcast_to(at[i][c], (8, LANES)), pick, axis=1
            ) * (1.0 / RADIUS)
        sum_ref[i] = jnp.zeros((64, LANES), F32)
    counts = [jnp.max(z_ref[g, 7:8, 0:LANES]).astype(I32) for g in range(groups)]
    most = functools.reduce(jnp.maximum, counts)
    source, target = iota((LANES, 2 * LANES), 0), iota((LANES, 2 * LANES), 1)
    same_half = source // 64 == target // 64
    prefix = flag(
        (target < LANES) & same_half & (source <= target)
        | (target >= LANES) & (source // 64 == target - LANES),
        BF16,
    )
    half = iota((TILES, LANES), 1) // 64

    def extract(source, g, start, block, shift):
        points = source[g, :, pl.ds(pl.multiple_of(start + block * LANES, LANES), LANES)]
        three = jnp.concatenate([p.astype(F32) for p in pieces(points, 3)], axis=0).astype(BF16)
        rank = rank_ref[pl.ds(pl.multiple_of((g * blocks + block) * TILES, TILES), TILES), :]
        entries = []
        for h in range(2):
            key = jnp.where(half == h, rank - shift, 0.0)
            chosen = jnp.concatenate([flag(key == s + 1.0) for s in range(SLOTS)], axis=0).astype(BF16)
            found = nt_dot(three, chosen)
            found = found[0:8] + found[8:16] + found[16:24]
            entries.append(jnp.where(iota((8, LANES), 0) < 4, found * (1.0 / RADIUS), found * 4.0))
        return entries

    def one_part(source, first, start, ahead):
        for g in range(groups):
            points = source[g, :, pl.ds(pl.multiple_of(start, LANES), run)]
            high, low = pieces(points, 2)
            both = jnp.concatenate([high.astype(F32), low.astype(F32), high.astype(F32)], axis=0)
            gap = jnp.dot(probe, both.astype(BF16), preferred_element_type=F32) + offset
            best = gap[0:TILES]
            for e in range(1, 8):
                best = jnp.minimum(best, gap[TILES * e : TILES * e + TILES])
            lane = iota((TILES, run), 1) + (ahead + start)
            hit = flag((best <= 0.0) & (lane >= first) & (lane < counts[g]))
            for b in range(blocks):
                hit_ref[(g * blocks + b) * TILES : (g * blocks + b + 1) * TILES, :] = hit[:, LANES * b : LANES * b + LANES]
        hits = hit_ref[...]
        ranks = jnp.dot(hits.astype(BF16), prefix, preferred_element_type=F32)
        rank_ref[...] = jnp.where(hits > 0.0, ranks[:, 0:LANES], -1000.0)
        filled = ranks[:, LANES:].reshape(groups * blocks, TILES, LANES)
        filled = jnp.max(filled, axis=1).astype(I32)
        over_ref[...] = filled
        copy = pltpu.make_async_copy(over_ref, over_smem, sem)
        copy.start()
        length = jnp.int32(0)
        for g in range(groups):
            inside = jnp.clip(counts[g] - (ahead + start), 0, run)
            for b in range(blocks):
                one, two = extract(source, g, start, b, 0.0)
                list_ref[length] = one
                length = length + jnp.where(inside > LANES * b, 1, 0)
                list_ref[length] = two
                length = length + jnp.where(inside > LANES * b + 64, 1, 0)
        def more(length):
            def block_more(index, length):
                g, b = index // blocks, index % blocks

                def round_more(r, length):
                    one, two = extract(source, g, start, b, (r * SLOTS).astype(F32))
                    list_ref[length] = one
                    length = length + jnp.where(over_smem[index, 0] > r * SLOTS, 1, 0)
                    list_ref[length] = two
                    length = length + jnp.where(over_smem[index, 1] > r * SLOTS, 1, 0)
                    return length

                rounds = (jnp.maximum(over_smem[index, 0], over_smem[index, 1]) + SLOTS - 1) // SLOTS
                return lax.fori_loop(1, rounds, round_more, length)

            for g in range(groups):
                crowd = [over_smem[g * blocks + b, h] for b in range(blocks) for h in range(2)]
                last = jnp.where(functools.reduce(jnp.maximum, crowd) > SLOTS, blocks, 0)
                length = lax.fori_loop(g * blocks, g * blocks + last, block_more, length)
            return length

        def four(step, carry):
            for i in range(2):
                for c in range(0, 64, 8):
                    total = [sum_ref[axis, c : c + 8, :] for axis in range(3)]
                    place = [corner_ref[axis, c : c + 8, :] for axis in range(3)]
                    for e in range(2):
                        entry = list_ref.at[4 * step + 2 * i + e]
                        gap = [place[axis] - entry[axis : axis + 1, :] for axis in range(3)]
                        square = gap[0] * gap[0] + gap[1] * gap[1] + gap[2] * gap[2]
                        ratio = square * lax.rsqrt(jnp.maximum(square, 1e-20))
                        inside = jnp.maximum(1.0 - ratio, 0.0)
                        inside = inside * inside
                        kernel = inside * inside * (ratio + 0.25)
                        for axis in range(3):
                            total[axis] = total[axis] + entry[4 + axis : 5 + axis, :] * kernel
                    for axis in range(3):
                        sum_ref[axis, c : c + 8, :] = total[axis]
            return carry

        def evaluate(length):
            for e in range(4):
                list_ref[length + e] = jnp.zeros((8, LANES), F32)
            lax.fori_loop(0, (length + 3) // 4, four, 0)

        evaluate(length)
        copy.wait()

        @pl.when(jnp.max(filled) > SLOTS)
        def crowded():
            evaluate(more(jnp.int32(0)))

    one_part(z_ref, 0, 0, 0)
    if far_ref is not None:
        step = min(run, far_ref.shape[2])

        def far_part(part, carry):
            first = (part - 1) * step
            one_part(far_ref, run + first, jnp.minimum(first, far_ref.shape[2] - step), run)
            return carry

        lax.fori_loop(1, 1 + (jnp.maximum(most - run, 0) + (step - 1)) // step, far_part, 0)
    spread = flag(iota((LANES, LANES), 0) % TILES == iota((LANES, LANES), 1) % TILES, BF16)
    own = iota((8, LANES), 0) == iota((8, LANES), 1) // TILES
    out = []
    for i in range(3):
        total = None
        for piece in pieces(sum_ref[i], 2):
            part = jnp.dot(piece, spread, preferred_element_type=F32)
            total = part if total is None else total + part
        rows = [
            jnp.sum(jnp.where(own, total[8 * c : 8 * c + 8], 0.0), axis=0, keepdims=True) for c in range(8)
        ]
        out.append(jnp.concatenate(rows, axis=0))
    return out


def radial_body(
    z_ref, far_ref, node_ref, derivs_ref, blend_ref, base_ref, start_ref, minus_inv_ref, count_ref, select_ref, send_ref,
    m_ref, where_ref, elem_0, elem_1,
    disp_ref, metric_ref, state_ref, trace_ref, p0, p1, p2, p3,
    corner_ref, hit_ref, rank_ref, list_ref, sum_ref, over_ref, over_smem, sem, nodes_ref, shift_ref, out_sem,
):
    packet_refs = (p0, p1, p2, p3)
    me, last = lax.axis_index("sub"), z_ref.shape[0] - 1
    sides = []
    for step in (-1, 1):
        peer, there = jnp.clip(me + step, 0, last), (me + step >= 0) & (me + step <= last)
        rows = [z_ref[peer, :, z_ref.shape[2] - PACKET + LANES * at :][:, 0:LANES] for at in range(3)]
        sides.append(jnp.where(there, jnp.concatenate(rows, axis=0), 0.0))
    base = base_ref[...] + from_neighbours(*sides, *in_line("elem", elem_0[...], elem_1[...]), where_ref, m_ref)
    corner = radial_displacement(
        z_ref, far_ref, node_ref, corner_ref, hit_ref, rank_ref, list_ref, sum_ref, over_ref, over_smem, sem
    )
    nodes_ref[...] = jnp.zeros_like(nodes_ref)
    for i in range(3):
        shift = pick_dot(blend_ref[...], corner[i], 2)
        shift_ref[i] = shift[0:27]
        nodes_ref[0:27, LANES * i : LANES * i + LANES] = node_ref[i] + shift[0:27]
    out = pltpu.make_async_copy(shift_ref, disp_ref, out_sem)
    out.start()
    jac = pick_dot(derivs_ref[...], nodes_ref[...], 3)
    j = [[jac[32 * l : 32 * l + 32, LANES * i : LANES * i + LANES] for l in range(3)] for i in range(3)]
    minor_a = j[1][1] * j[2][2] - j[1][2] * j[2][1]
    minor_b = j[1][0] * j[2][2] - j[1][2] * j[2][0]
    minor_c = j[1][0] * j[2][1] - j[1][1] * j[2][0]
    metric = 8.0 * (j[0][0] * minor_a - j[0][1] * minor_b + j[0][2] * minor_c)
    metric_ref[...] = jnp.zeros_like(metric_ref)
    for v in range(5):
        metric_ref[27 * v : 27 * v + 27, :] = metric[0:27]
    state = base + stored_dot(minus_inv_ref, metric_ref[...] * start_ref[...])
    finish(state, count_ref, select_ref, send_ref, state_ref, trace_ref, packet_refs)
    out.wait()


def finish(state, count_ref, select_ref, send_ref, state_ref, trace_ref, packet_refs):
    state = jnp.where(iota(state.shape, 1) < jnp.broadcast_to(count_ref[...], state.shape), state, 0.0)
    state_ref[...] = state
    traces = pick_dot(select_ref[...], state, 2)
    for f in range(6):
        trace_ref[f] = traces[48 * f : 48 * f + 48]
    tiles = [traces[48 * f : 48 * f + 48] for f in range(6)]
    left = iota((24, LANES), 1) < 64
    for pair in range(2):
        both = gather_columns(tiles, send_ref[pair : pair + 1, :], 0)
        top, bottom = both[0:24], both[24:48]
        ahead = jnp.where(left, top, pltpu.roll(bottom, 64, 1))
        back = jnp.where(left, pltpu.roll(top, 64, 1), bottom)
        odd = lax.axis_index(("sub", "elem")[pair]) % 2 == 1
        packet_refs[2 * pair][...] = jnp.where(odd, back, ahead)
        packet_refs[2 * pair + 1][...] = jnp.where(odd, ahead, back)


def gather_columns(tiles, index, first):
    rows = tiles[0].shape[0]
    tile = jnp.broadcast_to(index // LANES - first, (rows, LANES))
    lane = jnp.broadcast_to(index % LANES, (rows, LANES))
    out = jnp.zeros((rows, LANES), F32)
    for t, values in enumerate(tiles):
        out = jnp.where(tile == t, jnp.take_along_axis(values, lane, axis=1), out)
    return out


def in_line(axis, first, second):
    odd = lax.axis_index(axis) % 2 == 1
    return jnp.where(odd, first, second), jnp.where(odd, second, first)


def from_neighbours(before_sub, behind_sub, before_elem, behind_elem, where_ref, m_ref):
    packets = (before_sub, behind_sub, before_elem, behind_elem)
    columns = []
    for f in range(6):
        index = where_ref[f : f + 1, :] - 6 * LANES
        packet = jnp.broadcast_to(jnp.where(index >= 0, index // 64, -1), (24, LANES))
        lane = jnp.broadcast_to(index % 64, (24, LANES))
        halves = []
        for half in range(2):
            found = jnp.zeros((24, LANES), F32)
            for q, values in enumerate(packets):
                found = jnp.where(packet == q, jnp.take_along_axis(values, lane + 64 * half, axis=1), found)
            halves.append(found)
        columns += halves
    return stored_dot(m_ref, jnp.concatenate(columns, axis=0))


def arrived(sub_0, sub_1, elem_0, elem_1, where_ref, m_ref):
    sub = in_line("sub", sub_0[...], sub_1[...])
    return from_neighbours(*sub, *in_line("elem", elem_0[...], elem_1[...]), where_ref, m_ref)


def setup_body(
    u_ref, count_ref, select_in, send_ref, vol_ref, inv_ref, lift_ref, place_ref, right_ref, where_ref,
    node_in, derivs_in, blend_in,
    state_ref, trace_ref, p0, p1, p2, p3, held_ref, sent_ref, link_ref, node_ref, derivs_ref, blend_ref, select_ref, minus_ref, both_ref, m_ref, const_ref, base_ref,
    flat_ref, wide_ref,
):
    held_ref[...] = jnp.broadcast_to(count_ref[...], held_ref.shape)
    for q in range(4):
        sent_ref[q // 2 : q // 2 + 1, 64 * (q % 2) : 64 * (q % 2) + 64] = send_ref[0, q : q + 1, :]
    link_ref[...] = where_ref[...]
    node_ref[...] = node_in[...]
    derivs_ref[...] = derivs_in[...]
    blend_ref[...] = blend_in[...]
    select_ref[...] = select_in[...]
    flat_ref[...] = jnp.zeros_like(flat_ref)
    for v in range(5):
        flat_ref[27 * v : 27 * v + 27, :] = u_ref[v]
    finish(flat_ref[...], held_ref, select_ref, sent_ref, state_ref, trace_ref, (p0, p1, p2, p3))
    wide_ref[...] = jnp.zeros_like(wide_ref)
    wide_ref[0:135, 0:135] = inv_ref[...]
    inverse = wide_ref[:, 0:136]
    wide_ref[0:135, 0:135] = -split_dot(inv_ref[...], vol_ref[...])
    for k, piece in enumerate(pieces(-inverse, 2)):
        minus_ref[k] = piece
    for k, piece in enumerate(pieces(wide_ref[:, 0:136], 2)):
        both_ref[k] = piece
    coupling = split_dot(inverse[:, 0:135], lift_ref[...])
    moved = [jnp.dot(piece, place_ref[...], preferred_element_type=F32) for piece in pieces(coupling, 2)]
    for k in range(2):
        m_ref[k] = moved[k].astype(BF16)
    flat_ref[...] = jnp.zeros_like(flat_ref)
    for v in range(5):
        flat_ref[27 * v : 27 * v + 27, :] = right_ref[v]
    const = split_dot(inverse, flat_ref[...])
    const_ref[...] = const
    state = state_ref[...]
    base_ref[...] = state + const + stored_dot(both_ref, state) + local_part(trace_ref, where_ref, m_ref)


def local_part(trace_ref, where_ref, m_ref):
    tiles = [trace_ref[f] for f in range(6)]
    columns = [gather_columns(tiles, where_ref[f : f + 1, :], 0) for f in range(6)]
    return stored_dot(m_ref, jnp.concatenate(columns, axis=0))


def local_body(state_ref, trace_ref, metric_ref, const_ref, minus_ref, both_ref, m_ref, where_ref, out_ref):
    state = state_ref[...]
    out = state + const_ref[...] + stored_dot(both_ref, state)
    out = out + stored_dot(minus_ref, metric_ref[...] * state)
    out_ref[...] = out + local_part(trace_ref, where_ref, m_ref)


def sweep_body(
    base_ref, count_ref, select_ref, send_ref, m_ref, where_ref, sub_0, sub_1, elem_0, elem_1,
    state_ref, trace_ref, p0, p1, p2, p3,
):
    packet_refs = (p0, p1, p2, p3)
    state = base_ref[...] + arrived(sub_0, sub_1, elem_0, elem_1, where_ref, m_ref)
    finish(state, count_ref, select_ref, send_ref, state_ref, trace_ref, packet_refs)


def last_body(base_ref, count_ref, m_ref, where_ref, sub_0, sub_1, elem_0, elem_1, out_ref, state_ref):
    state = base_ref[...] + arrived(sub_0, sub_1, elem_0, elem_1, where_ref, m_ref)
    state_ref[...] = jnp.where(iota(state.shape, 1) < jnp.broadcast_to(count_ref[...], state.shape), state, 0.0)
    for v in range(5):
        out_ref[v] = state_ref[27 * v : 27 * v + 27, :]


def exchange(packets, axes=("sub", "elem")):
    out = []
    for axis in axes:
        first = 0 if axis == "sub" else 2
        size = lax.axis_size(axis)
        for turn in range(2):
            partner = [(i ^ 1) if turn == 0 else ((i + 1) ^ 1) - 1 for i in range(size)]
            pairs = [(i, j) for i, j in enumerate(partner) if 0 <= j < size]
            out.append(lax.ppermute(packets[first + turn], axis, pairs))
    return out


def spread(copies, axis):
    return lax.all_to_all(copies, axis, split_axis=0, concat_axis=0, tiled=True)


def radial_call(points, far, node_ref, derivs, blending, base, state, minus, elem_count, select, send, coupling, face_link, received):
    groups, _, run = points.shape
    blocks = (run - PACKET) // LANES * groups
    return call(
        radial_body,
        [shape_of(3, 27, LANES), shape_of(136, LANES), *STATE],
        [VMEM] * 15,
        [
            pltpu.VMEM((3, 64, LANES), F32),
            pltpu.VMEM((blocks * TILES, LANES), F32),
            pltpu.VMEM((blocks * TILES, LANES), F32),
            pltpu.VMEM((blocks * 16 + 8, 8, LANES), F32),
            pltpu.VMEM((3, 64, LANES), F32),
            pltpu.VMEM((blocks, LANES), I32),
            pltpu.SMEM((blocks, LANES), I32),
            pltpu.SemaphoreType.DMA,
            pltpu.VMEM((32, 3 * LANES), F32),
            pltpu.VMEM((3, 27, LANES), F32),
            pltpu.SemaphoreType.DMA,
        ],
        held=[False] + [True] * 7,
        out_specs=[pl.BlockSpec(memory_space=pl.ANY)] + [pl.BlockSpec(memory_space=VMEM)] * 7,
        name="radial",
    )(
        points, far, node_ref, derivs, blending, base, state, minus, elem_count, select, send,
        coupling, face_link, *received,
    )


def per_device(
    node_ref, cp_pos, cp_coef, cp_count, u_prev, right_side, elem_count, face_link, send_list,
    vol_block, block_inv, lift_matrix,
):
    derivs, blending, select, place = node_tables()
    derivs, blending = jnp.asarray(derivs, BF16), jnp.asarray(blending, BF16)
    select, place = jnp.asarray(select, BF16), jnp.asarray(place, BF16)
    n_elem, n_sub = lax.axis_size("elem"), lax.axis_size("sub")
    room = n_elem * cp_pos.shape[1]

    copies = call(
        payload_body, shape_of(n_elem, 2, LANES), [None] * 3, [pltpu.VMEM((8, LANES), F32)], name="payload"
    )(cp_count.reshape(1, 1), cp_pos, cp_coef)
    mine = spread(copies, "elem")
    *first, held_count, sent, link, held_node, held_derivs, held_blending, held_select, minus, both, coupling, const, base = call(
        setup_body,
        [
            *STATE, shape_of(1, LANES, dtype=I32), shape_of(2, LANES, dtype=I32), shape_of(6, LANES, dtype=I32),
            shape_of(*node_ref.shape), shape_of(*derivs.shape, dtype=BF16), shape_of(*blending.shape, dtype=BF16),
            shape_of(*select.shape, dtype=BF16),
            shape_of(2, 136, 136, dtype=BF16), shape_of(2, 136, 136, dtype=BF16), shape_of(2, 136, 288, dtype=BF16),
            shape_of(136, LANES), shape_of(136, LANES),
        ],
        [None, None, HBM, None] + [HBM] * 9,
        [pltpu.VMEM((136, LANES), F32), pltpu.VMEM((136, 256), F32)],
        name="setup",
    )(
        u_prev, elem_count.reshape(1, 1), select, send_list, vol_block, block_inv, lift_matrix, place, right_side, face_link,
        node_ref, derivs, blending,
    )
    state, traces, *packets = first
    near = min(RUN, room)
    gathered, rest = call(
        compact_body,
        [shape_of(n_sub, 8, near + PACKET), shape_of(n_sub, 8, max(room - near, near))],
        [VMEM] * 4,
        [pltpu.VMEM((n_elem, 7 * LANES), BF16)],
        name="compact",
    )(mine, packets[0], packets[1], base)
    points = spread(gathered, "sub")
    received = exchange(packets, ("elem",))
    far = lax.cond(jnp.max(points[:, 7, 0]) > near, lambda x: spread(x, "sub"), lambda x: x, rest)
    displacement, metric, state, traces, *packets = radial_call(
        points, far, held_node, held_derivs, held_blending, base, state, minus, held_count, held_select, sent,
        coupling, link, received,
    )
    for sweep in range(1, ITERS):
        received = exchange(packets)
        base = call(local_body, shape_of(136, LANES), [VMEM] * 8, name="local")(
            state, traces, metric, const, minus, both, coupling, link
        )
        if sweep < ITERS - 1:
            state, traces, *packets = call(sweep_body, STATE, [VMEM] * 10, name="sweep")(
                base, held_count, held_select, sent, coupling, link, *received
            )
        else:
            solution_out = call(
                last_body,
                shape_of(5, 27, LANES),
                [VMEM] * 8,
                [pltpu.VMEM((136, LANES), F32)],
                held=False,
                name="last",
            )(base, held_count, coupling, link, *received)
    return displacement, solution_out


def solution(mesh):
    in_specs = (
        P(None, None, BOTH), P(None, BOTH), P(None, BOTH), P(BOTH), P(None, None, BOTH), P(None, None, BOTH),
        P(BOTH), P(None, BOTH), P(BOTH, None, None), P(), P(), P(),
    )
    out_specs = (P(None, None, BOTH), P(None, None, BOTH))
    return jax.shard_map(per_device, mesh=mesh, in_specs=in_specs, out_specs=out_specs, check_vma=False)
```

```python
import functools

import jax
import jax.numpy as jnp
import numpy as np
from jax import lax
from jax.experimental import pallas as pl
from jax.experimental.pallas import tpu as pltpu
from jax.sharding import PartitionSpec as P

ITERS = 3
BOTH = ("elem", "sub")
RADIUS = 1.5
FAR = 1000.0
LANES = 128
STRIP = 256
HEAD = 640
RUN = 768
PACKET = 384
TILES = 16
SLOTS = 8
INTERPRET = False
F32, BF16, I32 = jnp.float32, jnp.bfloat16, jnp.int32
VMEM = pltpu.MemorySpace.VMEM
HBM = pltpu.MemorySpace.HBM


def node_tables():
    slopes = np.array([[-1.5, 2.0, -0.5], [-0.5, 0.0, 0.5], [0.5, -2.0, 1.5]])
    one = np.eye(3)
    derivs = np.zeros((96, 32), np.float32)
    for axis, full in enumerate(
        (
            np.kron(one, np.kron(one, slopes)),
            np.kron(one, np.kron(slopes, one)),
            np.kron(slopes, np.eye(9)),
        )
    ):
        derivs[32 * axis : 32 * axis + 27, :27] = full
    blending = np.zeros((32, 8), np.float32)
    for node in range(27):
        place = (node % 3 - 1.0, node // 3 % 3 - 1.0, node // 9 - 1.0)
        for corner in range(8):
            weight = 1.0
            for axis in range(3):
                side = 1.0 if corner >> axis & 1 else -1.0
                weight *= (1.0 + side * place[axis]) / 2.0
            blending[node, corner] = weight
    select = np.zeros((288, 136), np.float32)
    for face in range(6):
        axis, layer = face // 2, 2 * (face % 2)
        nodes = [n for n in range(27) if n // 3**axis % 3 == layer]
        for var in range(5):
            for at, node in enumerate(nodes):
                select[48 * face + 9 * var + at, 27 * var + node] = 1.0
    place = np.zeros((270, 288), np.float32)
    for face in range(6):
        for entry in range(45):
            place[6 * entry + face, 48 * face + entry] = 1.0
    return derivs, blending, select, place


CORNERS = [2 * (c & 1) + 6 * (c >> 1 & 1) + 18 * (c >> 2) for c in range(8)]


def pieces(x, count):
    out = []
    for _ in range(count):
        piece = x.astype(BF16)
        out.append(piece)
        x = x - piece.astype(F32)
    return out


def stored_dot(a_ref, b):
    b1, b2 = pieces(b, 2)
    high = jnp.dot(a_ref[0], b1, preferred_element_type=F32)
    return high + (jnp.dot(a_ref[0], b2, preferred_element_type=F32) + jnp.dot(a_ref[1], b1, preferred_element_type=F32))


def split_dot(a, b):
    a1, a2 = pieces(a, 2)
    b1, b2 = pieces(b, 2)
    high = jnp.dot(a1, b1, preferred_element_type=F32)
    return high + (jnp.dot(a1, b2, preferred_element_type=F32) + jnp.dot(a2, b1, preferred_element_type=F32))


def pick_dot(a, b, count=2):
    out = None
    for piece in pieces(b, count):
        part = jnp.dot(a, piece, preferred_element_type=F32)
        out = part if out is None else out + part
    return out


def nt_dot(a, b):
    return lax.dot_general(a, b, (((1,), (1,)), ((), ())), preferred_element_type=F32)


def iota(shape, dim):
    return lax.broadcasted_iota(I32, shape, dim)


def flag(mask, dtype=F32):
    return jnp.where(mask, 1.0, 0.0).astype(dtype)


def call(body, out_shape, in_spaces, scratch=(), held=True, in_specs=None, out_specs=None, **kw):
    held = held if isinstance(held, list) else jax.tree.map(lambda _: held, out_shape)

    def place(s, stays):
        return pltpu.VMEM(s.shape, s.dtype) if stays and not INTERPRET else s

    run = pl.pallas_call(
        body,
        out_shape=jax.tree.map(place, out_shape, held),
        in_specs=in_specs or [pl.BlockSpec(memory_space=VMEM) for _ in in_spaces],
        out_specs=out_specs or jax.tree.map(lambda _: pl.BlockSpec(memory_space=VMEM), out_shape),
        scratch_shapes=list(scratch),
        interpret=INTERPRET,
        **kw,
    )

    def placed(*args):
        if INTERPRET:
            return run(*args)
        return run(*[a if s is None else pltpu.with_memory_space_constraint(a, s) for a, s in zip(args, in_spaces, strict=True)])

    return placed


def shape_of(*dims, dtype=F32):
    return jax.ShapeDtypeStruct(dims, dtype)


STATE = [shape_of(136, LANES), shape_of(6, 48, LANES), *[shape_of(24, LANES)] * 4]


def payload_body(count_ref, pos_ref, coef_ref, out_ref, row_ref):
    count = jnp.broadcast_to(count_ref[...], (1, LANES))[:, 0:32]
    live = iota((1, 32), 1) < count
    for axis in range(3):
        lanes = slice(32 * axis, 32 * axis + 32)
        row_ref[0:1, lanes] = jnp.where(live, pos_ref[axis : axis + 1, :], FAR)
        row_ref[1:2, lanes] = jnp.where(live, coef_ref[axis : axis + 1, :], 0.0)
    row_ref[0:1, 96:128] = jnp.zeros((1, 32), F32)
    row_ref[1:2, 96:128] = count.astype(F32)
    out_ref[...] = jnp.broadcast_to(row_ref[0:2, :][None], out_ref.shape)


def compact_body(in_ref, p0, p1, order_ref, out_ref, far_ref, part_ref):
    owners = in_ref.shape[0]
    copies, _, near = out_ref.shape
    near = near - PACKET
    me = lax.axis_index("sub")
    odd = me % 2 == 1
    ahead, back = jnp.where(odd, p1[...], p0[...]), jnp.where(odd, p0[...], p1[...])
    for peer in range(copies):
        for at in range(3):
            lanes = slice(near + LANES * at, near + LANES * at + LANES)
            rows = slice(8 * at, 8 * at + 8)
            out_ref[peer, :, lanes] = jnp.where(peer > me, ahead[rows], back[rows])
    first, second = in_ref[:, 0, :], in_ref[:, 1, :]
    wide = jnp.broadcast_to(second[:, 96:97], (owners, LANES))
    below = flag(iota((owners, owners), 1) < iota((owners, owners), 0), BF16)
    above = flag(iota((owners, owners), 0) < iota((owners, owners), 1), BF16)
    start_col = jnp.dot(below, wide.astype(BF16), preferred_element_type=F32)
    pick = flag(iota((8, LANES), 1) == 96, BF16)
    count_row = nt_dot(pick, second.astype(BF16))
    start_row = jnp.dot(count_row.astype(BF16), above, preferred_element_type=F32)
    low, end = start_row[0:1, :], (start_row + count_row)[0:1, :]
    total = jnp.max(end, axis=1, keepdims=True)
    for at, piece in enumerate(pieces(first, 3)):
        part_ref[:, LANES * at : LANES * at + LANES] = piece
    for at, piece in enumerate(pieces(second, 2) + pieces(start_col, 2)):
        part_ref[:, LANES * (3 + at) : LANES * (4 + at)] = piece
    feature, group = iota((8, LANES), 0), iota((8, LANES), 1) // 32
    fold_first = flag((feature < 3) & (feature == group), BF16)
    fold_second = flag((feature > 3) & (feature < 7) & (feature == group + 4), BF16)

    def one_strip(base, strip, target, at):
        slot = (iota((strip, LANES), 1) % 32).astype(F32)
        place = (iota((strip, owners), 0) + base).astype(F32)
        owner = flag((place >= low) & (place < end), BF16)
        found = jnp.dot(owner, part_ref[...], preferred_element_type=F32)
        start = found[:, 5 * LANES : 6 * LANES] + found[:, 6 * LANES :]
        here = (iota((strip, LANES), 0) + base).astype(F32)
        mine = slot == here - start
        out = None
        for k in range(3):
            a = jnp.where(mine, found[:, LANES * k : LANES * k + LANES], 0.0).astype(BF16)
            both = nt_dot(fold_first, a)
            if k < 2:
                b = jnp.where(mine, found[:, LANES * (3 + k) : LANES * (4 + k)], 0.0).astype(BF16)
                both = both + nt_dot(fold_second, b)
            out = both if out is None else out + both
        dead = (iota((8, strip), 1) + base).astype(F32) >= total
        row = iota((8, strip), 0)
        out = jnp.where(dead, jnp.where(row < 3, FAR, 0.0), out)
        square = jnp.sum(jnp.where(row < 3, out * out, 0.0), axis=0, keepdims=True)
        out = jnp.where(row == 3, square, out)
        out = jnp.where(row == 7, total, out)
        target[:, :, at : at + strip] = jnp.broadcast_to(out[None], (copies, 8, strip))

    head = min(HEAD, near)
    one_strip(0, head, out_ref, 0)
    if head < near or far_ref is not None:
        count = jnp.max(total)
    if head < near:

        @pl.when(count > head)
        def second():
            one_strip(head, near - head, out_ref, head)

    if far_ref is not None:
        for at in range(0, far_ref.shape[2], STRIP):

            @pl.when(count > near + at)
            def further(at=at):
                one_strip(near + at, min(STRIP, far_ref.shape[2] - at), far_ref, at)


def radial_displacement(z_ref, far_ref, node_ref, corner_ref, hit_ref, rank_ref, list_ref, sum_ref, over_ref, over_smem, sem):
    groups, _, run = z_ref.shape
    run = run - PACKET
    blocks = run // LANES
    at = [[node_ref[i, k : k + 1, :] for k in CORNERS] for i in range(3)]
    middle, reach = [], [None] * 8
    for i in range(3):
        low = functools.reduce(jnp.minimum, at[i])
        high = functools.reduce(jnp.maximum, at[i])
        middle.append(0.5 * (low + high))
        for c in range(8):
            gap = (at[i][c] - middle[i]) ** 2
            reach[c] = gap if i == 0 else reach[c] + gap
    limit = RADIUS + jnp.sqrt(functools.reduce(jnp.maximum, reach))
    offset = middle[0] ** 2 + middle[1] ** 2 + middle[2] ** 2 - limit * limit * 1.001 - 0.2
    row = iota((LANES, LANES), 0)
    table = jnp.where((row == 3) | (row == 11), 1.0, 0.0)
    for i in range(3):
        high, low = (p.astype(F32) for p in pieces(-2.0 * middle[i], 2))
        table = jnp.where((row == i) | (row == 8 + i), high, jnp.where(row == 16 + i, low, table))
    probe = jnp.transpose(table)[:, 0:24].astype(BF16)
    offset = jnp.transpose(jnp.broadcast_to(offset, (LANES, LANES)))
    offset = jnp.concatenate([offset] * blocks, axis=1)
    pick = iota((8, LANES), 0) * TILES + iota((8, LANES), 1) % TILES
    for i in range(3):
        for c in range(8):
            corner_ref[i, 8 * c : 8 * c + 8, :] = jnp.take_along_axis(
                jnp.broadcast_to(at[i][c], (8, LANES)), pick, axis=1
            ) * (1.0 / RADIUS)
        sum_ref[i] = jnp.zeros((64, LANES), F32)
    counts = [jnp.max(z_ref[g, 7:8, 0:LANES]).astype(I32) for g in range(groups)]
    most = functools.reduce(jnp.maximum, counts)
    source, target = iota((LANES, 2 * LANES), 0), iota((LANES, 2 * LANES), 1)
    same_half = source // 64 == target // 64
    prefix = flag(
        (target < LANES) & same_half & (source <= target)
        | (target >= LANES) & (source // 64 == target - LANES),
        BF16,
    )
    half = iota((TILES, LANES), 1) // 64

    def extract(source, g, start, block, shift):
        points = source[g, :, pl.ds(pl.multiple_of(start + block * LANES, LANES), LANES)]
        three = jnp.concatenate([p.astype(F32) for p in pieces(points, 3)], axis=0).astype(BF16)
        rank = rank_ref[pl.ds(pl.multiple_of((g * blocks + block) * TILES, TILES), TILES), :]
        entries = []
        for h in range(2):
            key = jnp.where(half == h, rank - shift, 0.0)
            chosen = jnp.concatenate([flag(key == s + 1.0) for s in range(SLOTS)], axis=0).astype(BF16)
            found = nt_dot(three, chosen)
            found = found[0:8] + found[8:16] + found[16:24]
            entries.append(jnp.where(iota((8, LANES), 0) < 4, found * (1.0 / RADIUS), found * 4.0))
        return entries

    def one_part(source, first, start, ahead):
        for g in range(groups):
            points = source[g, :, pl.ds(pl.multiple_of(start, LANES), run)]
            high, low = pieces(points, 2)
            both = jnp.concatenate([high.astype(F32), low.astype(F32), high.astype(F32)], axis=0)
            gap = jnp.dot(probe, both.astype(BF16), preferred_element_type=F32) + offset
            best = gap[0:TILES]
            for e in range(1, 8):
                best = jnp.minimum(best, gap[TILES * e : TILES * e + TILES])
            lane = iota((TILES, run), 1) + (ahead + start)
            hit = flag((best <= 0.0) & (lane >= first) & (lane < counts[g]))
            for b in range(blocks):
                hit_ref[(g * blocks + b) * TILES : (g * blocks + b + 1) * TILES, :] = hit[:, LANES * b : LANES * b + LANES]
        hits = hit_ref[...]
        ranks = jnp.dot(hits.astype(BF16), prefix, preferred_element_type=F32)
        rank_ref[...] = jnp.where(hits > 0.0, ranks[:, 0:LANES], -1000.0)
        filled = ranks[:, LANES:].reshape(groups * blocks, TILES, LANES)
        filled = jnp.max(filled, axis=1).astype(I32)
        over_ref[...] = filled
        copy = pltpu.make_async_copy(over_ref, over_smem, sem)
        copy.start()
        length = jnp.int32(0)
        for g in range(groups):
            inside = jnp.clip(counts[g] - (ahead + start), 0, run)
            for b in range(blocks):
                one, two = extract(source, g, start, b, 0.0)
                list_ref[length] = one
                length = length + jnp.where(inside > LANES * b, 1, 0)
                list_ref[length] = two
                length = length + jnp.where(inside > LANES * b + 64, 1, 0)
        def more(length):
            def block_more(index, length):
                g, b = index // blocks, index % blocks

                def round_more(r, length):
                    one, two = extract(source, g, start, b, (r * SLOTS).astype(F32))
                    list_ref[length] = one
                    length = length + jnp.where(over_smem[index, 0] > r * SLOTS, 1, 0)
                    list_ref[length] = two
                    length = length + jnp.where(over_smem[index, 1] > r * SLOTS, 1, 0)
                    return length

                rounds = (jnp.maximum(over_smem[index, 0], over_smem[index, 1]) + SLOTS - 1) // SLOTS
                return lax.fori_loop(1, rounds, round_more, length)

            for g in range(groups):
                crowd = [over_smem[g * blocks + b, h] for b in range(blocks) for h in range(2)]
                last = jnp.where(functools.reduce(jnp.maximum, crowd) > SLOTS, blocks, 0)
                length = lax.fori_loop(g * blocks, g * blocks + last, block_more, length)
            return length

        def four(step, carry):
            for c in range(0, 64, 8):
                total = [sum_ref[axis, c : c + 8, :] for axis in range(3)]
                place = [corner_ref[axis, c : c + 8, :] for axis in range(3)]
                for e in range(4):
                    entry = list_ref.at[4 * step + e]
                    gap = [place[axis] - entry[axis : axis + 1, :] for axis in range(3)]
                    square = gap[0] * gap[0] + gap[1] * gap[1] + gap[2] * gap[2]
                    ratio = square * lax.rsqrt(jnp.maximum(square, 1e-20))
                    inside = jnp.maximum(1.0 - ratio, 0.0)
                    inside = inside * inside
                    kernel = inside * inside * (ratio + 0.25)
                    for axis in range(3):
                        total[axis] = total[axis] + entry[4 + axis : 5 + axis, :] * kernel
                for axis in range(3):
                    sum_ref[axis, c : c + 8, :] = total[axis]
            return carry

        def evaluate(length):
            for e in range(4):
                list_ref[length + e] = jnp.zeros((8, LANES), F32)
            lax.fori_loop(0, (length + 3) // 4, four, 0)

        evaluate(length)
        copy.wait()

        @pl.when(jnp.max(filled) > SLOTS)
        def crowded():
            evaluate(more(jnp.int32(0)))

    one_part(z_ref, 0, 0, 0)
    if far_ref is not None:
        step = min(run, far_ref.shape[2])

        def far_part(part, carry):
            first = (part - 1) * step
            one_part(far_ref, run + first, jnp.minimum(first, far_ref.shape[2] - step), run)
            return carry

        lax.fori_loop(1, 1 + (jnp.maximum(most - run, 0) + (step - 1)) // step, far_part, 0)
    spread = flag(iota((LANES, LANES), 0) % TILES == iota((LANES, LANES), 1) % TILES, BF16)
    own = iota((8, LANES), 0) == iota((8, LANES), 1) // TILES
    out = []
    for i in range(3):
        total = None
        for piece in pieces(sum_ref[i], 2):
            part = jnp.dot(piece, spread, preferred_element_type=F32)
            total = part if total is None else total + part
        rows = [
            jnp.sum(jnp.where(own, total[8 * c : 8 * c + 8], 0.0), axis=0, keepdims=True) for c in range(8)
        ]
        out.append(jnp.concatenate(rows, axis=0))
    return out


def radial_body(
    z_ref, far_ref, node_ref, derivs_ref, blend_ref, base_ref, start_ref, minus_inv_ref, count_ref, select_ref, send_ref,
    m_ref, where_ref, elem_0, elem_1,
    disp_ref, metric_ref, state_ref, trace_ref, p0, p1, p2, p3,
    corner_ref, hit_ref, rank_ref, list_ref, sum_ref, over_ref, over_smem, sem, nodes_ref, shift_ref, out_sem,
):
    packet_refs = (p0, p1, p2, p3)
    me, last = lax.axis_index("sub"), z_ref.shape[0] - 1
    sides = []
    for step in (-1, 1):
        peer, there = jnp.clip(me + step, 0, last), (me + step >= 0) & (me + step <= last)
        rows = [z_ref[peer, :, z_ref.shape[2] - PACKET + LANES * at :][:, 0:LANES] for at in range(3)]
        sides.append(jnp.where(there, jnp.concatenate(rows, axis=0), 0.0))
    base = base_ref[...] + from_neighbours(*sides, *in_line("elem", elem_0[...], elem_1[...]), where_ref, m_ref)
    corner = radial_displacement(
        z_ref, far_ref, node_ref, corner_ref, hit_ref, rank_ref, list_ref, sum_ref, over_ref, over_smem, sem
    )
    nodes_ref[...] = jnp.zeros_like(nodes_ref)
    for i in range(3):
        shift = pick_dot(blend_ref[...], corner[i], 2)
        shift_ref[i] = shift[0:27]
        nodes_ref[0:27, LANES * i : LANES * i + LANES] = node_ref[i] + shift[0:27]
    out = pltpu.make_async_copy(shift_ref, disp_ref, out_sem)
    out.start()
    jac = pick_dot(derivs_ref[...], nodes_ref[...], 3)
    j = [[jac[32 * l : 32 * l + 32, LANES * i : LANES * i + LANES] for l in range(3)] for i in range(3)]
    minor_a = j[1][1] * j[2][2] - j[1][2] * j[2][1]
    minor_b = j[1][0] * j[2][2] - j[1][2] * j[2][0]
    minor_c = j[1][0] * j[2][1] - j[1][1] * j[2][0]
    metric = 8.0 * (j[0][0] * minor_a - j[0][1] * minor_b + j[0][2] * minor_c)
    metric_ref[...] = jnp.zeros_like(metric_ref)
    for v in range(5):
        metric_ref[27 * v : 27 * v + 27, :] = metric[0:27]
    state = base + stored_dot(minus_inv_ref, metric_ref[...] * start_ref[...])
    finish(state, count_ref, select_ref, send_ref, state_ref, trace_ref, packet_refs)
    out.wait()


def finish(state, count_ref, select_ref, send_ref, state_ref, trace_ref, packet_refs):
    state = jnp.where(iota(state.shape, 1) < jnp.broadcast_to(count_ref[...], state.shape), state, 0.0)
    state_ref[...] = state
    traces = pick_dot(select_ref[...], state, 2)
    for f in range(6):
        trace_ref[f] = traces[48 * f : 48 * f + 48]
    tiles = [traces[48 * f : 48 * f + 48] for f in range(6)]
    left = iota((24, LANES), 1) < 64
    for pair in range(2):
        both = gather_columns(tiles, send_ref[pair : pair + 1, :], 0)
        top, bottom = both[0:24], both[24:48]
        ahead = jnp.where(left, top, pltpu.roll(bottom, 64, 1))
        back = jnp.where(left, pltpu.roll(top, 64, 1), bottom)
        odd = lax.axis_index(("sub", "elem")[pair]) % 2 == 1
        packet_refs[2 * pair][...] = jnp.where(odd, back, ahead)
        packet_refs[2 * pair + 1][...] = jnp.where(odd, ahead, back)


def gather_columns(tiles, index, first):
    rows = tiles[0].shape[0]
    tile = jnp.broadcast_to(index // LANES - first, (rows, LANES))
    lane = jnp.broadcast_to(index % LANES, (rows, LANES))
    out = jnp.zeros((rows, LANES), F32)
    for t, values in enumerate(tiles):
        out = jnp.where(tile == t, jnp.take_along_axis(values, lane, axis=1), out)
    return out


def in_line(axis, first, second):
    odd = lax.axis_index(axis) % 2 == 1
    return jnp.where(odd, first, second), jnp.where(odd, second, first)


def from_neighbours(before_sub, behind_sub, before_elem, behind_elem, where_ref, m_ref):
    packets = (before_sub, behind_sub, before_elem, behind_elem)
    columns = []
    for f in range(6):
        index = where_ref[f : f + 1, :] - 6 * LANES
        packet = jnp.broadcast_to(jnp.where(index >= 0, index // 64, -1), (24, LANES))
        lane = jnp.broadcast_to(index % 64, (24, LANES))
        halves = []
        for half in range(2):
            found = jnp.zeros((24, LANES), F32)
            for q, values in enumerate(packets):
                found = jnp.where(packet == q, jnp.take_along_axis(values, lane + 64 * half, axis=1), found)
            halves.append(found)
        columns += halves
    return stored_dot(m_ref, jnp.concatenate(columns, axis=0))


def arrived(sub_0, sub_1, elem_0, elem_1, where_ref, m_ref):
    sub = in_line("sub", sub_0[...], sub_1[...])
    return from_neighbours(*sub, *in_line("elem", elem_0[...], elem_1[...]), where_ref, m_ref)


def setup_body(
    u_ref, count_ref, select_in, send_ref, vol_ref, inv_ref, lift_ref, place_ref, right_ref, where_ref,
    node_in, derivs_in, blend_in,
    state_ref, trace_ref, p0, p1, p2, p3, held_ref, sent_ref, link_ref, node_ref, derivs_ref, blend_ref, select_ref, minus_ref, both_ref, m_ref, const_ref, base_ref,
    flat_ref, wide_ref,
):
    held_ref[...] = jnp.broadcast_to(count_ref[...], held_ref.shape)
    for q in range(4):
        sent_ref[q // 2 : q // 2 + 1, 64 * (q % 2) : 64 * (q % 2) + 64] = send_ref[0, q : q + 1, :]
    link_ref[...] = where_ref[...]
    node_ref[...] = node_in[...]
    derivs_ref[...] = derivs_in[...]
    blend_ref[...] = blend_in[...]
    select_ref[...] = select_in[...]
    flat_ref[...] = jnp.zeros_like(flat_ref)
    for v in range(5):
        flat_ref[27 * v : 27 * v + 27, :] = u_ref[v]
    finish(flat_ref[...], held_ref, select_ref, sent_ref, state_ref, trace_ref, (p0, p1, p2, p3))
    wide_ref[...] = jnp.zeros_like(wide_ref)
    wide_ref[0:135, 0:135] = inv_ref[...]
    inverse = wide_ref[:, 0:136]
    wide_ref[0:135, 0:135] = -split_dot(inv_ref[...], vol_ref[...])
    for k, piece in enumerate(pieces(-inverse, 2)):
        minus_ref[k] = piece
    for k, piece in enumerate(pieces(wide_ref[:, 0:136], 2)):
        both_ref[k] = piece
    coupling = split_dot(inverse[:, 0:135], lift_ref[...])
    moved = [jnp.dot(piece, place_ref[...], preferred_element_type=F32) for piece in pieces(coupling, 2)]
    for k in range(2):
        m_ref[k] = moved[k].astype(BF16)
    flat_ref[...] = jnp.zeros_like(flat_ref)
    for v in range(5):
        flat_ref[27 * v : 27 * v + 27, :] = right_ref[v]
    const = split_dot(inverse, flat_ref[...])
    const_ref[...] = const
    state = state_ref[...]
    base_ref[...] = state + const + stored_dot(both_ref, state) + local_part(trace_ref, where_ref, m_ref)


def local_part(trace_ref, where_ref, m_ref):
    tiles = [trace_ref[f] for f in range(6)]
    columns = [gather_columns(tiles, where_ref[f : f + 1, :], 0) for f in range(6)]
    return stored_dot(m_ref, jnp.concatenate(columns, axis=0))


def local_body(state_ref, trace_ref, metric_ref, const_ref, minus_ref, both_ref, m_ref, where_ref, out_ref):
    state = state_ref[...]
    out = state + const_ref[...] + stored_dot(both_ref, state)
    out = out + stored_dot(minus_ref, metric_ref[...] * state)
    out_ref[...] = out + local_part(trace_ref, where_ref, m_ref)


def sweep_body(
    base_ref, count_ref, select_ref, send_ref, m_ref, where_ref, sub_0, sub_1, elem_0, elem_1,
    state_ref, trace_ref, p0, p1, p2, p3,
):
    packet_refs = (p0, p1, p2, p3)
    state = base_ref[...] + arrived(sub_0, sub_1, elem_0, elem_1, where_ref, m_ref)
    finish(state, count_ref, select_ref, send_ref, state_ref, trace_ref, packet_refs)


def last_body(base_ref, count_ref, m_ref, where_ref, sub_0, sub_1, elem_0, elem_1, out_ref, state_ref):
    state = base_ref[...] + arrived(sub_0, sub_1, elem_0, elem_1, where_ref, m_ref)
    state_ref[...] = jnp.where(iota(state.shape, 1) < jnp.broadcast_to(count_ref[...], state.shape), state, 0.0)
    for v in range(5):
        out_ref[v] = state_ref[27 * v : 27 * v + 27, :]


def exchange(packets, axes=("sub", "elem")):
    out = []
    for axis in axes:
        first = 0 if axis == "sub" else 2
        size = lax.axis_size(axis)
        for turn in range(2):
            partner = [(i ^ 1) if turn == 0 else ((i + 1) ^ 1) - 1 for i in range(size)]
            pairs = [(i, j) for i, j in enumerate(partner) if 0 <= j < size]
            out.append(lax.ppermute(packets[first + turn], axis, pairs))
    return out


def spread(copies, axis):
    return lax.all_to_all(copies, axis, split_axis=0, concat_axis=0, tiled=True)


def radial_call(points, far, node_ref, derivs, blending, base, state, minus, elem_count, select, send, coupling, face_link, received):
    groups, _, run = points.shape
    blocks = (run - PACKET) // LANES * groups
    return call(
        radial_body,
        [shape_of(3, 27, LANES), shape_of(136, LANES), *STATE],
        [VMEM] * 15,
        [
            pltpu.VMEM((3, 64, LANES), F32),
            pltpu.VMEM((blocks * TILES, LANES), F32),
            pltpu.VMEM((blocks * TILES, LANES), F32),
            pltpu.VMEM((blocks * 16 + 8, 8, LANES), F32),
            pltpu.VMEM((3, 64, LANES), F32),
            pltpu.VMEM((blocks, LANES), I32),
            pltpu.SMEM((blocks, LANES), I32),
            pltpu.SemaphoreType.DMA,
            pltpu.VMEM((32, 3 * LANES), F32),
            pltpu.VMEM((3, 27, LANES), F32),
            pltpu.SemaphoreType.DMA,
        ],
        held=[False] + [True] * 7,
        out_specs=[pl.BlockSpec(memory_space=pl.ANY)] + [pl.BlockSpec(memory_space=VMEM)] * 7,
        name="radial",
    )(
        points, far, node_ref, derivs, blending, base, state, minus, elem_count, select, send,
        coupling, face_link, *received,
    )


def per_device(
    node_ref, cp_pos, cp_coef, cp_count, u_prev, right_side, elem_count, face_link, send_list,
    vol_block, block_inv, lift_matrix,
):
    derivs, blending, select, place = node_tables()
    derivs, blending = jnp.asarray(derivs, BF16), jnp.asarray(blending, BF16)
    select, place = jnp.asarray(select, BF16), jnp.asarray(place, BF16)
    n_elem, n_sub = lax.axis_size("elem"), lax.axis_size("sub")
    room = n_elem * cp_pos.shape[1]

    copies = call(
        payload_body, shape_of(n_elem, 2, LANES), [None] * 3, [pltpu.VMEM((8, LANES), F32)], name="payload"
    )(cp_count.reshape(1, 1), cp_pos, cp_coef)
    mine = spread(copies, "elem")
    *first, held_count, sent, link, held_node, held_derivs, held_blending, held_select, minus, both, coupling, const, base = call(
        setup_body,
        [
            *STATE, shape_of(1, LANES, dtype=I32), shape_of(2, LANES, dtype=I32), shape_of(6, LANES, dtype=I32),
            shape_of(*node_ref.shape), shape_of(*derivs.shape, dtype=BF16), shape_of(*blending.shape, dtype=BF16),
            shape_of(*select.shape, dtype=BF16),
            shape_of(2, 136, 136, dtype=BF16), shape_of(2, 136, 136, dtype=BF16), shape_of(2, 136, 288, dtype=BF16),
            shape_of(136, LANES), shape_of(136, LANES),
        ],
        [None, None, HBM, None] + [HBM] * 9,
        [pltpu.VMEM((136, LANES), F32), pltpu.VMEM((136, 256), F32)],
        name="setup",
    )(
        u_prev, elem_count.reshape(1, 1), select, send_list, vol_block, block_inv, lift_matrix, place, right_side, face_link,
        node_ref, derivs, blending,
    )
    state, traces, *packets = first
    near = min(RUN, room)
    gathered, rest = call(
        compact_body,
        [shape_of(n_sub, 8, near + PACKET), shape_of(n_sub, 8, max(room - near, near))],
        [VMEM] * 4,
        [pltpu.VMEM((n_elem, 7 * LANES), BF16)],
        name="compact",
    )(mine, packets[0], packets[1], base)
    points = spread(gathered, "sub")
    received = exchange(packets, ("elem",))
    far = lax.cond(jnp.max(points[:, 7, 0]) > near, lambda x: spread(x, "sub"), lambda x: x, rest)
    displacement, metric, state, traces, *packets = radial_call(
        points, far, held_node, held_derivs, held_blending, base, state, minus, held_count, held_select, sent,
        coupling, link, received,
    )
    for sweep in range(1, ITERS):
        received = exchange(packets)
        base = call(local_body, shape_of(136, LANES), [VMEM] * 8, name="local")(
            state, traces, metric, const, minus, both, coupling, link
        )
        if sweep < ITERS - 1:
            state, traces, *packets = call(sweep_body, STATE, [VMEM] * 10, name="sweep")(
                base, held_count, held_select, sent, coupling, link, *received
            )
        else:
            solution_out = call(
                last_body,
                shape_of(5, 27, LANES),
                [VMEM] * 8,
                [pltpu.VMEM((136, LANES), F32)],
                held=False,
                name="last",
            )(base, held_count, coupling, link, *received)
    return displacement, solution_out


def solution(mesh):
    in_specs = (
        P(None, None, BOTH), P(None, BOTH), P(None, BOTH), P(BOTH), P(None, None, BOTH), P(None, None, BOTH),
        P(BOTH), P(None, BOTH), P(BOTH, None, None), P(), P(), P(),
    )
    out_specs = (P(None, None, BOTH), P(None, None, BOTH))
    return jax.shard_map(per_device, mesh=mesh, in_specs=in_specs, out_specs=out_specs, check_vma=False)
```
